256 devices in a mesh: ctx: 64 (over z, x, core), head: 4 (over y).
Axes of the slice: x: 4, y: 4, z: 8, core: 2. Of those that a mesh axis runs over, the one named last changes fastest.
Arguments:
- queries: bfloat16 [16384, 4096], P('ctx', 'head'), may hold values from -6 to 6
- keys: bfloat16 [16384, 2, 4096], P('ctx', None, 'head'), may hold values from -6 to 6
- values: bfloat16 [16384, 2, 4096], P('ctx', None, 'head'), may hold values from -6 to 6
- betas: float32 [2, 32, 16384], P(None, 'head', 'ctx'), may hold values from 0.02 to 1.9
- log_decay: float32 [32, 16384], P('head', 'ctx'), may hold values from -1 to 0
- segment: int32 [16384], P('ctx'), may hold values from 0 to 127, never falling along the last dimension, each value on 1 to 2048 neighbouring positions
- gain: float32 [4096], P('head'), may hold values from 0.1 to 1.9
- out_weight: bfloat16 [4096, 4096], P('head'), may hold values from -0.125 to 0.125
Outputs:
- mixed: bfloat16 [16384, 4096], P('ctx', 'head')
The draws below stay inside these ranges and needn't reach their ends.
Inputs may be any that keep to these rules, and one draw needn't show every extreme that they name: `segment`: document numbers never fall along the context; every document has 1 to 2048 tokens and one has exactly 2048.
All inputs are finite; a program needn't handle non-finite values.
Results may differ from the reference program's by a relative error of at most 0.0049.
Values sent between devices are 32-bit elements; how exact they have to be, the bound alone decides.
No kernel may reach another device: no remote copies, remote signals or barrier semaphores. Data moves between devices by JAX's collectives and lax.ppermute only.
A program may use at most 192 MiB of HBM per device.

```python
import math
import jax
import jax.numpy as jnp
import numpy as np
from jax import lax

D = 4096
H = 32
DK = 128
DV = 128
GROUP = 64
TOK_DEV = 256
TOTAL_POSITIONS = 16384
DOCUMENT_LIMIT = 2048
DOCS = 128


def slow_heads(key, slow_count):
    order = jax.random.permutation(jax.random.fold_in(key, 101), H)
    return order < slow_count


def draw_keys(key, part):
    blocks = TOTAL_POSITIONS // GROUP
    shared_key, noise_key = jax.random.split(jax.random.fold_in(key, 17))
    shared = jnp.clip(jax.random.normal(shared_key, (blocks, 1, 1, H, DK), jnp.float32), -4.0, 4.0)
    noise = jnp.clip(jax.random.normal(noise_key, (blocks, GROUP, 2, H, DK), jnp.float32), -4.0, 4.0)
    combined = 0.6 * shared + 0.8 * noise
    return combined.reshape(TOTAL_POSITIONS, 2, H * DK).astype(jnp.bfloat16)


def draw_betas(key, part):
    slow_count = H // 2
    fast_low = 0.2
    upper_fast_rate = 1.8
    slow = slow_heads(key, slow_count)
    first, second = jax.random.split(jax.random.fold_in(key, 5))
    weak = jnp.exp(jax.random.uniform(first, (2, H, TOTAL_POSITIONS), jnp.float32, math.log(0.02), math.log(0.049)))
    strong = jax.random.uniform(second, (2, H, TOTAL_POSITIONS), jnp.float32, fast_low, upper_fast_rate)
    return jnp.where(slow[None, :, None], weak, strong).astype(jnp.float32)


def draw_log_decay(key, part):
    slow_count = H // 2
    slow = slow_heads(key, slow_count)
    packed_keys = jax.random.split(jax.random.fold_in(key, 9), 6)
    slow_rate = jnp.exp(jax.random.uniform(packed_keys[0], (H,), jnp.float32, math.log(2e-05), math.log(0.0001)))
    fast_rate = jnp.exp(jax.random.uniform(packed_keys[1], (H,), jnp.float32, math.log(0.001), math.log(0.004)))
    base = jnp.where(slow, slow_rate, fast_rate)
    blocks = TOTAL_POSITIONS // TOK_DEV
    factor = jnp.exp(jax.random.uniform(packed_keys[2], (H, blocks), jnp.float32, -math.log(2.0), math.log(2.0)))
    factor = jnp.repeat(factor, TOK_DEV, axis=1)
    rough = jax.random.uniform(packed_keys[3], (H, TOTAL_POSITIONS), jnp.float32, 0.5, 1.5)
    token_group = jax.random.uniform(packed_keys[4], (TOTAL_POSITIONS,), jnp.float32) < 2.0 / DOCUMENT_LIMIT
    token_total = jax.random.uniform(packed_keys[5], (TOTAL_POSITIONS,), jnp.float32, 0.22, 0.69)
    forget_factor = jnp.where(token_group, token_total, jnp.zeros_like(token_total))
    return (-(base[:, None] * factor * rough) - forget_factor[None, :]).astype(jnp.float32)


def spiked(entries, own_key, source, target, shards_of, factor):
    def block_of(axis_at):
        return (jnp.arange(entries.shape[axis_at]) // (entries.shape[axis_at] // shards_of)).reshape((-1,) + (1,) * (entries.ndim - 1 - axis_at))

    first = jax.random.permutation(own_key, shards_of)[block_of(target)]
    second = (block_of(target) + shards_of // 2) % shards_of
    return jnp.where((block_of(source) == first) | (block_of(source) == second), factor * entries, entries)


def steps_of(stream_key, shape, shards, low, top_value):
    loudness, own = 1.0, jax.random.fold_in(stream_key, 6)
    for position, blocks in shards:
        draws = jnp.exp(jax.random.uniform(jax.random.fold_in(own, position), (blocks,), jnp.float32, low / len(shards), top_value / len(shards)))
        loudness = loudness * jnp.repeat(draws, shape[position] // blocks).reshape([-1 if axis == position else 1 for axis in range(len(shape))])
    return loudness


def profile(count, total, limit, slope):
    portions = [(1 << 20) // math.isqrt(rank ** slope) + 1 for rank in range(2, count + 1)]
    surplus, holding = total - limit - (count - 1), [1] * (count - 1)
    while surplus > 0:
        free = [i for i in range(count - 1) if holding[i] < limit]
        pool, budget = sum([portions[i] for i in free]), surplus
        for i in free:
            more = min(limit - holding[i], max(1, budget * portions[i] // pool), surplus)
            holding[i] = holding[i] + more
            surplus = surplus - more
    return np.array([limit] + holding)


def ragged_sizes(key, number_of, total, most, slope):
    if number_of == 2:
        one = jax.random.randint(key, (), max(1, total - most), min(most, total - 1) + 1)
        return jnp.stack([one, total - one])
    tallies = jnp.asarray(profile(number_of, total, most, slope), jnp.int32)
    twos = (number_of - 1) // 2
    source_of, receiver = tallies[1:1 + 2 * twos:2], tallies[2:2 + 2 * twos:2]
    slack = jnp.minimum(source_of - 1, most - receiver)
    moved = jax.random.randint(jax.random.fold_in(key, 1), (twos,), 0, 1 << 20) % (slack + 1)
    tallies = tallies.at[1:1 + 2 * twos:2].set(source_of - moved).at[2:2 + 2 * twos:2].set(receiver + moved)
    return tallies[jax.random.permutation(jax.random.fold_in(key, 2), number_of)]


def normal_values(rng, extent, scale, most, pieces=(), dtype=jnp.bfloat16):
    level = steps_of(rng, extent, pieces, -0.22, 0.18) if pieces else 1.0
    drawn = jax.random.normal(rng, extent, jnp.float32) * scale * level
    return jnp.minimum(jnp.maximum(drawn, -most), most).astype(dtype)


def gaussian_with(own_key, shape, scale, limit, shards, heavy, held_as=jnp.bfloat16):
    array = scale * jax.random.normal(own_key, shape, jnp.float32)
    if shards:
        array = array * steps_of(own_key, shape, shards, -0.22, 0.18)
    return jnp.clip(spiked(array, jax.random.fold_in(own_key, 3), *heavy), -limit, limit).astype(held_as)


def setup_inputs(seed: int = 0) -> dict:
    arg_keys = jax.random.split(jax.random.key(seed), 9)
    return {
        "queries": normal_values(arg_keys[0], (TOTAL_POSITIONS, H * DK), 1.0, 6.0, ((0, 64), (1, 4))),
        "keys": draw_keys(jax.random.fold_in(arg_keys[8], 71), 0),
        "values": normal_values(arg_keys[2], (TOTAL_POSITIONS, 2, H * DV), 1.0, 6.0, ((0, 64), (2, 4))),
        "betas": draw_betas(jax.random.fold_in(arg_keys[8], 71), 0),
        "log_decay": draw_log_decay(jax.random.fold_in(arg_keys[8], 71), 0),
        "segment": jnp.searchsorted(jnp.cumsum(ragged_sizes(arg_keys[5], DOCS, TOTAL_POSITIONS, DOCUMENT_LIMIT, 2)), jnp.arange(TOTAL_POSITIONS), side="right").astype(jnp.int32),
        "gain": jnp.clip(1.0 + 0.18 * jax.random.normal(arg_keys[6], (H * DV,), jnp.float32), 0.1, 1.9),
        "out_weight": gaussian_with(arg_keys[7], (H * DV, D), (H * DV) ** -0.5, 0.125, ((0, 4),), (0, 1, 4, 2.0)),
    }


def unit_rows(matrix):
    return matrix / jnp.sqrt(lax.optimization_barrier(jnp.sum(matrix * matrix, axis=-1, keepdims=True)) + 1e-06)

def reference(queries, keys, values, betas, log_decay, segment, gain, out_weight):
    positions = queries.shape[0]
    highest = lax.Precision.HIGHEST
    query_unit = unit_rows(queries.astype(jnp.float32).reshape(positions, H, DK))
    key_unit = unit_rows(keys.astype(jnp.float32).reshape(positions, 2, H, DK))
    value_rows = values.astype(jnp.float32).reshape(positions, 2, H, DV)
    strengths = jnp.transpose(betas, (2, 0, 1))
    decay = jnp.exp(log_decay).T
    previous = jnp.concatenate([jnp.full((1,), -1, jnp.int32), segment[:-1].astype(jnp.int32)])
    retain_all = jnp.where((segment.astype(jnp.int32) == previous)[:, None], decay, jnp.zeros_like(decay))

    def advance(state, inputs):
        retain, query_row, key_pair, value_pair, strength_pair = inputs
        state = state * retain[:, None, None]
        for which in range(2):
            guess = jnp.einsum('hvk,hk->hv', state, key_pair[which], precision=highest)
            update = jnp.einsum('hv,hk->hvk', value_pair[which] - guess, key_pair[which], precision=highest)
            state = state + strength_pair[which][:, None, None] * update
        reading = jnp.einsum('hvk,hk->hv', state, query_row, precision=highest)
        return (state, reading)
    blank_state = jnp.zeros((H, DV, DK), jnp.float32)
    final_state, attended = lax.scan(advance, blank_state, (retain_all, query_unit, key_unit, value_rows, strengths))
    inverse_rms = 1.0 / jnp.sqrt(lax.optimization_barrier(jnp.mean(attended * attended, axis=-1, keepdims=True)) + 1e-06)
    normed = ((attended * inverse_rms).reshape(positions, H * DV) * gain[None, :]).astype(jnp.bfloat16)
    return jnp.dot(normed, out_weight, preferred_element_type=jnp.float32).astype(jnp.bfloat16)
```

```python
import jax
import jax.numpy as jnp
from jax import lax
from jax.experimental import pallas as pl
from jax.experimental.pallas import tpu as pltpu
from jax.sharding import PartitionSpec as P

DK = 128
DV = 128
GROUP = 64
ROWS = 2 * GROUP
DOCUMENT_LIMIT = 2048
EPS = 1e-06
F32 = jnp.float32
BF16 = jnp.bfloat16


def dotf(a, b, dims=(((1,), (0,)), ((), ()))):
    return lax.dot_general(a, b, dims, preferred_element_type=F32)


def halves(x):
    hi = x.astype(BF16)
    lo = (x - hi.astype(F32)).astype(BF16)
    return hi, lo


def side(x):
    return jnp.concatenate(halves(x), axis=1)


def mm(a, b):
    left = side(a)
    outs = []
    for c in range(0, b.shape[1], 128):
        right = side(b[:, c : c + 128])
        r = dotf(left, jnp.concatenate([right, right], axis=0))
        outs.append(r[:, :128] + r[:, 128:])
    return outs[0] if len(outs) == 1 else jnp.concatenate(outs, axis=1)


def mm_exact_right(a, b16):
    return dotf(side(a), jnp.concatenate([b16, b16], axis=0))


def iota(shape, dim):
    return lax.broadcasted_iota(jnp.int32, shape, dim)


def invert(systems):
    r, c = iota((ROWS, ROWS), 0), iota((ROWS, ROWS), 1)
    eye = (r == c).astype(F32)
    pair = (r >> 1) == (c >> 1)
    xs = [eye - jnp.where(pair, s, 0.0) for s in systems]
    shift = 1
    while (1 << shift) < ROWS:
        band = ((r >> (shift + 1)) == (c >> (shift + 1))) & ((r >> shift) != (c >> shift))
        ys = [mm(jnp.where(band, s, 0.0), x) for s, x in zip(systems, xs)]
        xs = [x - mm(x, y) for x, y in zip(xs, ys)]
        shift += 1
    return xs


def local_kernel(heads_step, blocks, q_ref, k_ref, v_ref, beta_ref, log_ref, seg_ref,
                 pair_ref, out_ref, map_ref, tab_ref):
    step = pl.program_id(0)
    heads = log_ref.shape[0]

    @pl.when(step == 0)
    def _():
        t, s = iota((GROUP, ROWS), 0), iota((GROUP, ROWS), 1)
        even = (s == 2 * t).astype(F32)
        odd = (s == 2 * t + 1).astype(F32)
        upto = (t <= (s >> 1)).astype(F32)
        flat = (t <= s).astype(F32)
        same = (s == t).astype(F32)
        both = even + odd

        def pick(x, sel):
            return lax.dot_general(x, sel, (((1,), (0,)), ((), ())),
                                   precision=lax.Precision.HIGHEST, preferred_element_type=F32)

        seg = jnp.broadcast_to(seg_ref[...].astype(F32), (heads, blocks * GROUP))
        for n in range(blocks):
            cut = slice(n * GROUP, (n + 1) * GROUP)
            lg = log_ref[:, cut]
            tab_ref[:, 8 * n, :] = pick(lg, upto)
            tab_ref[:, 8 * n + 1, :] = pick(beta_ref[0, :, cut], even) + pick(beta_ref[1, :, cut], odd)
            tab_ref[:, 8 * n + 2, :] = pick(seg[:, cut], both)
            tab_ref[:, 8 * n + 3, :] = pick(lg, flat)
            tab_ref[:, 8 * n + 4, :] = pick(seg[:, cut], same)
            for z in range(5, 8):
                tab_ref[:, 8 * n + z, :] = jnp.zeros((heads, ROWS), F32)

    r, c = iota((ROWS, ROWS), 0), iota((ROWS, ROWS), 1)
    diag = r == c
    eye = diag.astype(F32)
    strictly = r > c
    qr, qc = iota((GROUP, ROWS), 0), iota((GROUP, ROWS), 1)
    seen = qc <= 2 * qr + 1

    items = []
    for g in range(heads_step):
        lanes = slice(g * DK, (g + 1) * DK)
        table = tab_ref[step * heads_step + g]
        columns = jnp.concatenate([table[8 * n : 8 * n + 8] for n in range(blocks)]
                                  + [jnp.zeros((ROWS - 8 * blocks, ROWS), F32)], axis=0).T
        prior = table[2:3, 0:1]
        for n in range(blocks):
            key = k_ref[n * ROWS : (n + 1) * ROWS, lanes]
            query = q_ref[n * GROUP : (n + 1) * GROUP, lanes]
            value = v_ref[n * ROWS : (n + 1) * ROWS, lanes]
            cum_row, beta_row, seg_row = (table[8 * n + i : 8 * n + i + 1] for i in range(3))
            cum_col, beta_col, seg_col = (columns[:, 8 * n + i : 8 * n + i + 1] for i in range(3))
            cum_q, seg_q = (columns[:GROUP, 8 * n + i : 8 * n + i + 1] for i in (3, 4))
            cum_last, seg_last = cum_row[:, ROWS - 1 :], seg_row[:, ROWS - 1 :]
            gram = dotf(jnp.concatenate([key, query], axis=0), key, (((1,), (1,)), ((), ())))
            raw, raw_q = gram[:ROWS], gram[ROWS:]
            own = jnp.where(diag, raw, 0.0)
            rk_row = lax.rsqrt(jnp.sum(own, axis=0, keepdims=True) + EPS)
            rk_col = lax.rsqrt(jnp.sum(own, axis=1, keepdims=True) + EPS)
            query32 = query.astype(F32)
            rq = lax.rsqrt(jnp.sum(query32 * query32, axis=1, keepdims=True) + EPS)
            grow_row = rk_row * jnp.exp(-cum_row)
            system = jnp.where(strictly & (seg_col == seg_row), raw, 0.0) * (
                beta_col * rk_col * jnp.exp(cum_col)) * grow_row
            scores = jnp.where(seen & (seg_q == seg_row), raw_q, 0.0) * (rq * jnp.exp(cum_q)) * grow_row
            entry_row = jnp.where(seg_row == prior, jnp.exp(cum_row), 0.0)
            entry_q = jnp.where(seg_q == prior, jnp.exp(cum_q), 0.0)
            tail_col = jnp.where(seg_col == seg_last, jnp.exp(cum_last - cum_col), 0.0) * rk_col
            tail_entry = jnp.where(seg_last == prior, jnp.exp(cum_last), 0.0)
            items.append(dict(
                g=g, n=n, key=key, value=value, system=system, scores=scores,
                reach=query32 * (rq * entry_q), wv=beta_row, wk=beta_row * rk_row * entry_row,
                tail=tail_col, tail_entry=tail_entry))
            prior = seg_last

    for item, x in zip(items, invert([item["system"] for item in items])):
        pseudo = mm_exact_right(x * item["wv"], item["value"])
        key_mix = mm_exact_right(x * item["wk"], item["key"])
        both = jnp.concatenate([key_mix, pseudo], axis=1)
        item["both"] = both
    for item in items:
        hi, lo = halves(item["both"] * item["tail"])
        r2 = dotf(item["key"], jnp.concatenate([hi, lo], axis=1), (((0,), (0,)), ((), ())))
        r2 = r2[:, : 2 * DK] + r2[:, 2 * DK :]
        item["trans"] = item["tail_entry"] * eye - r2[:, :DK]
        item["add"] = r2[:, DK:]
        inner = mm(item["scores"], item["both"])
        item["reach"] = item["reach"] - inner[:, :DK]
        item["local"] = inner[:, DK:]

    for n in range(blocks):
        for g in range(heads_step):
            item = items[g * blocks + n]
            rows = slice(n * GROUP, (n + 1) * GROUP)
            lanes = slice(g * DV, (g + 1) * DV)
            if n == 0:
                map_ref[rows, lanes] = item["reach"]
                out_ref[rows, lanes] = item["local"]
                item["prefix"] = jnp.concatenate([item["trans"], item["add"]], axis=1)
            else:
                prefix = items[g * blocks + n - 1]["prefix"]
                joined = mm(jnp.concatenate([item["reach"], item["trans"]], axis=0), prefix)
                map_ref[rows, lanes] = joined[:GROUP, :DK]
                out_ref[rows, lanes] = item["local"] + joined[:GROUP, DK:]
                item["prefix"] = jnp.concatenate(
                    [joined[GROUP:, :DK], joined[GROUP:, DK:] + item["add"]], axis=1)
            if n == blocks - 1:
                pair_ref[g, :DK, :] = item["prefix"]
    first = seg_ref[:, 0:1].astype(F32)
    last = seg_ref[:, blocks * GROUP - 1 :].astype(F32)
    ends = jnp.where(iota((8, 2 * DK), 0) == 0, first, last)
    for g in range(heads_step):
        pair_ref[g, DK:, :] = ends


def local_stage(queries, keys, values, betas, log_decay, segment):
    tok, heads = queries.shape[0], betas.shape[1]
    blocks = tok // GROUP
    step = 1
    body = lambda *refs: local_kernel(step, blocks, *refs)
    return pl.pallas_call(
        body,
        grid=(heads // step,),
        in_specs=[
            pl.BlockSpec((tok, step * DK), lambda h: (0, h)),
            pl.BlockSpec((2 * tok, step * DK), lambda h: (0, h)),
            pl.BlockSpec((2 * tok, step * DV), lambda h: (0, h)),
            pl.BlockSpec((2, heads, tok), lambda h: (0, 0, 0)),
            pl.BlockSpec((heads, tok), lambda h: (0, 0)),
            pl.BlockSpec((1, tok), lambda h: (0, 0)),
        ],
        out_specs=[
            pl.BlockSpec((step, DK + 8, DK + DV), lambda h: (h, 0, 0)),
            pl.BlockSpec((tok, step * DV), lambda h: (0, h)),
            pl.BlockSpec((tok, step * DK), lambda h: (0, h)),
        ],
        out_shape=[
            jax.ShapeDtypeStruct((heads, DK + 8, DK + DV), F32),
            jax.ShapeDtypeStruct((tok, heads * DV), F32),
            jax.ShapeDtypeStruct((tok, heads * DK), F32),
        ],
        scratch_shapes=[pltpu.VMEM((heads, 8 * blocks, ROWS), F32)],
        compiler_params=pltpu.CompilerParams(dimension_semantics=("arbitrary",)),
        name="local_stage",
    )(queries, keys.reshape(2 * tok, heads * DK), values.reshape(2 * tok, heads * DV),
      betas, log_decay, segment.reshape(1, tok))


def prefix_kernel(in_ref, ex_ref, end_ref):
    count = in_ref.shape[0]
    flags = [jnp.where(in_ref[i, DK : DK + 1, :] == in_ref[i - 1, DK + 1 : DK + 2, :], 1.0, 0.0)
             for i in range(1, count)]
    maps = [in_ref[i, :DK, :DK] * (1.0 if i == 0 else flags[i - 1][:, :DK]) for i in range(count)]
    adds = [in_ref[i, :DK, DK:] for i in range(count)]
    width = 1
    while width < count:
        new_maps, new_adds = list(maps), list(adds)
        for i in range(count):
            if i & width:
                j = (i // width) * width - 1
                joined = mm(maps[i], jnp.concatenate([maps[j], adds[j]], axis=1))
                new_maps[i] = joined[:, :DK]
                new_adds[i] = joined[:, DK:] + adds[i]
        maps, adds = new_maps, new_adds
        width *= 2
    r, c = iota((DK, DK), 0), iota((DK, DK), 1)
    ex_ref[0, :, :DK] = (r == c).astype(F32)
    ex_ref[0, :, DK:] = jnp.zeros((DK, DV), F32)
    for i in range(1, count):
        ex_ref[i, :, :DK] = maps[i - 1] * flags[i - 1][:, :DK]
        ex_ref[i, :, DK:] = adds[i - 1] * flags[i - 1][:, DK:]
    end_ref[:DK, :] = adds[count - 1]
    end_ref[DK:, :] = in_ref[count - 1, DK:, :DV]


def incoming_kernel(in_ref, ex_ref, end_ref, out_ref):
    flag = jnp.where(in_ref[0, DK : DK + 1, :DV] == end_ref[DK + 1 : DK + 2, :], 1.0, 0.0)
    state = end_ref[:DK, :] * flag
    for i in range(ex_ref.shape[0]):
        out_ref[i] = mm(ex_ref[i, :, :DK], state) + ex_ref[i, :, DK:]


def final_kernel(local_ref, map_ref, state_ref, gain_ref, weight_ref, out_ref, normed_ref):
    heads = state_ref.shape[0]

    @pl.when(pl.program_id(0) == 0)
    def _():
        for h in range(heads):
            lanes = slice(h * DV, (h + 1) * DV)
            attended = local_ref[:, lanes] + mm(map_ref[:, lanes], state_ref[h])
            mean = jnp.mean(attended * attended, axis=1, keepdims=True)
            normed_ref[:, lanes] = (attended * lax.rsqrt(mean + EPS) * gain_ref[:, lanes]).astype(BF16)

    out_ref[...] = dotf(normed_ref[...], weight_ref[...])


def final_stage(local, mapped, state, gain, weight):
    tok, feats = local.shape
    heads, width = state.shape[0], weight.shape[1]
    tile = min(width, 512)
    whole = lambda *shape: pl.BlockSpec(shape, lambda j: (0,) * len(shape))
    return pl.pallas_call(
        final_kernel,
        grid=(width // tile,),
        in_specs=[whole(tok, feats), whole(tok, feats), whole(heads, DK, DV), whole(1, feats),
                  pl.BlockSpec((feats, tile), lambda j: (0, j))],
        out_specs=pl.BlockSpec((tok, tile), lambda j: (0, j)),
        out_shape=jax.ShapeDtypeStruct((tok, width), F32),
        scratch_shapes=[pltpu.VMEM((tok, feats), BF16)],
        compiler_params=pltpu.CompilerParams(dimension_semantics=("arbitrary",)),
        name="final_stage",
    )(local, mapped, state, gain.reshape(1, feats), weight)


def shards(queries, keys, values, betas, log_decay, segment, gain, out_weight):
    tok, heads = queries.shape[0], betas.shape[1]
    devices = lax.axis_size("ctx")
    span = DOCUMENT_LIMIT // tok
    assert span == heads and devices % span == 0
    groups = [list(range(i, i + span)) for i in range(0, devices, span)]
    pair, local, mapped = local_stage(queries, keys, values, betas, log_decay, segment)
    mine = lax.all_to_all(pair, "ctx", 0, 0, axis_index_groups=groups)
    exclusive, end = pl.pallas_call(
        prefix_kernel,
        out_shape=[jax.ShapeDtypeStruct((span, DK, DK + DV), F32),
                   jax.ShapeDtypeStruct((DK + 8, DV), F32)],
        name="prefix_stage",
    )(mine)
    end = lax.ppermute(end, "ctx", [(i, i + span) for i in range(devices - span)])
    states = pl.pallas_call(
        incoming_kernel,
        out_shape=jax.ShapeDtypeStruct((span, DK, DV), F32),
        name="incoming_stage",
    )(mine, exclusive, end)
    states = lax.all_to_all(states, "ctx", 0, 0, axis_index_groups=groups)
    terms = final_stage(local, mapped, states, gain, out_weight)
    return lax.psum_scatter(terms, "head", scatter_dimension=1, tiled=True).astype(BF16)


def solution(mesh):
    return jax.shard_map(
        shards,
        mesh=mesh,
        in_specs=(
            P("ctx", "head"),
            P("ctx", None, "head"),
            P("ctx", None, "head"),
            P(None, "head", "ctx"),
            P("head", "ctx"),
            P("ctx"),
            P("head"),
            P("head", None),
        ),
        out_specs=P("ctx", "head"),
        check_vma=False,
    )
```

```python
import jax
import jax.numpy as jnp
from jax import lax
from jax.experimental import pallas as pl
from jax.experimental.pallas import tpu as pltpu
from jax.sharding import PartitionSpec as P

DK = 128
DV = 128
GROUP = 64
ROWS = 2 * GROUP
DOCUMENT_LIMIT = 2048
EPS = 1e-06
F32 = jnp.float32
BF16 = jnp.bfloat16


def dotf(a, b, dims=(((1,), (0,)), ((), ()))):
    return lax.dot_general(a, b, dims, preferred_element_type=F32)


def halves(x):
    hi = x.astype(BF16)
    lo = (x - hi.astype(F32)).astype(BF16)
    return hi, lo


def side(x):
    return jnp.concatenate(halves(x), axis=1)


def mm(a, b):
    left = side(a)
    outs = []
    for c in range(0, b.shape[1], 128):
        right = side(b[:, c : c + 128])
        r = dotf(left, jnp.concatenate([right, right], axis=0))
        outs.append(r[:, :128] + r[:, 128:])
    return outs[0] if len(outs) == 1 else jnp.concatenate(outs, axis=1)


def mm_exact_right(a, b16):
    return dotf(side(a), jnp.concatenate([b16, b16], axis=0))


def iota(shape, dim):
    return lax.broadcasted_iota(jnp.int32, shape, dim)


def invert(systems):
    r, c = iota((ROWS, ROWS), 0), iota((ROWS, ROWS), 1)
    eye = (r == c).astype(F32)
    pair = (r >> 1) == (c >> 1)
    xs = [eye - jnp.where(pair, s, 0.0) for s in systems]
    shift = 1
    while (1 << shift) < ROWS:
        band = ((r >> (shift + 1)) == (c >> (shift + 1))) & ((r >> shift) != (c >> shift))
        ys = [mm(jnp.where(band, s, 0.0), x) for s, x in zip(systems, xs)]
        xs = [x - mm(x, y) for x, y in zip(xs, ys)]
        shift += 1
    return xs


def local_kernel(heads_step, blocks, q_ref, k_ref, v_ref, beta_ref, log_ref, seg_ref,
                 pair_ref, out_ref, map_ref, tab_ref):
    step = pl.program_id(0)
    heads = log_ref.shape[0]

    @pl.when(step == 0)
    def _():
        t, s = iota((GROUP, ROWS), 0), iota((GROUP, ROWS), 1)
        even = (s == 2 * t).astype(F32)
        odd = (s == 2 * t + 1).astype(F32)
        upto = (t <= (s >> 1)).astype(F32)
        flat = (t <= s).astype(F32)
        same = (s == t).astype(F32)
        both = even + odd

        def pick(x, sel):
            return lax.dot_general(x, sel, (((1,), (0,)), ((), ())),
                                   precision=lax.Precision.HIGHEST, preferred_element_type=F32)

        seg = jnp.broadcast_to(seg_ref[...].astype(F32), (heads, blocks * GROUP))
        for n in range(blocks):
            cut = slice(n * GROUP, (n + 1) * GROUP)
            lg = log_ref[:, cut]
            tab_ref[:, 8 * n, :] = pick(lg, upto)
            tab_ref[:, 8 * n + 1, :] = pick(beta_ref[0, :, cut], even) + pick(beta_ref[1, :, cut], odd)
            tab_ref[:, 8 * n + 2, :] = pick(seg[:, cut], both)
            tab_ref[:, 8 * n + 3, :] = pick(lg, flat)
            tab_ref[:, 8 * n + 4, :] = pick(seg[:, cut], same)
            for z in range(5, 8):
                tab_ref[:, 8 * n + z, :] = jnp.zeros((heads, ROWS), F32)

    r, c = iota((ROWS, ROWS), 0), iota((ROWS, ROWS), 1)
    diag = r == c
    eye = diag.astype(F32)
    strictly = r > c
    qr, qc = iota((GROUP, ROWS), 0), iota((GROUP, ROWS), 1)
    seen = qc <= 2 * qr + 1

    items = []
    for g in range(heads_step):
        lanes = slice(g * DK, (g + 1) * DK)
        table = tab_ref[step * heads_step + g]
        columns = jnp.concatenate([table[8 * n : 8 * n + 8] for n in range(blocks)]
                                  + [jnp.zeros((ROWS - 8 * blocks, ROWS), F32)], axis=0).T
        prior = table[2:3, 0:1]
        for n in range(blocks):
            key = k_ref[n * GROUP : (n + 1) * GROUP, :, lanes].reshape(ROWS, DK)
            query = q_ref[n * GROUP : (n + 1) * GROUP, lanes]
            value = v_ref[n * GROUP : (n + 1) * GROUP, :, lanes].reshape(ROWS, DV)
            cum_row, beta_row, seg_row = (table[8 * n + i : 8 * n + i + 1] for i in range(3))
            cum_col, beta_col, seg_col = (columns[:, 8 * n + i : 8 * n + i + 1] for i in range(3))
            cum_q, seg_q = (columns[:GROUP, 8 * n + i : 8 * n + i + 1] for i in (3, 4))
            cum_last, seg_last = cum_row[:, ROWS - 1 :], seg_row[:, ROWS - 1 :]
            gram = dotf(jnp.concatenate([key, query], axis=0), key, (((1,), (1,)), ((), ())))
            raw, raw_q = gram[:ROWS], gram[ROWS:]
            own = jnp.where(diag, raw, 0.0)
            rk_row = lax.rsqrt(jnp.sum(own, axis=0, keepdims=True) + EPS)
            rk_col = lax.rsqrt(jnp.sum(own, axis=1, keepdims=True) + EPS)
            query32 = query.astype(F32)
            rq = lax.rsqrt(jnp.sum(query32 * query32, axis=1, keepdims=True) + EPS)
            grow_row = rk_row * jnp.exp(-cum_row)
            system = jnp.where(strictly & (seg_col == seg_row), raw, 0.0) * (
                beta_col * rk_col * jnp.exp(cum_col)) * grow_row
            scores = jnp.where(seen & (seg_q == seg_row), raw_q, 0.0) * (rq * jnp.exp(cum_q)) * grow_row
            entry_row = jnp.where(seg_row == prior, jnp.exp(cum_row), 0.0)
            entry_q = jnp.where(seg_q == prior, jnp.exp(cum_q), 0.0)
            tail_col = jnp.where(seg_col == seg_last, jnp.exp(cum_last - cum_col), 0.0) * rk_col
            tail_entry = jnp.where(seg_last == prior, jnp.exp(cum_last), 0.0)
            items.append(dict(
                g=g, n=n, key=key, value=value, system=system, scores=scores,
                reach=query32 * (rq * entry_q), wv=beta_row, wk=beta_row * rk_row * entry_row,
                tail=tail_col, tail_entry=tail_entry))
            prior = seg_last

    for item, x in zip(items, invert([item["system"] for item in items])):
        pseudo = mm_exact_right(x * item["wv"], item["value"])
        key_mix = mm_exact_right(x * item["wk"], item["key"])
        both = jnp.concatenate([key_mix, pseudo], axis=1)
        item["both"] = both
    for item in items:
        hi, lo = halves(item["both"] * item["tail"])
        r2 = dotf(item["key"], jnp.concatenate([hi, lo], axis=1), (((0,), (0,)), ((), ())))
        r2 = r2[:, : 2 * DK] + r2[:, 2 * DK :]
        item["trans"] = item["tail_entry"] * eye - r2[:, :DK]
        item["add"] = r2[:, DK:]
        inner = mm(item["scores"], item["both"])
        item["reach"] = item["reach"] - inner[:, :DK]
        item["local"] = inner[:, DK:]

    for n in range(blocks):
        for g in range(heads_step):
            item = items[g * blocks + n]
            rows = slice(n * GROUP, (n + 1) * GROUP)
            lanes = slice(g * DV, (g + 1) * DV)
            if n == 0:
                map_ref[rows, lanes] = item["reach"]
                out_ref[rows, lanes] = item["local"]
                item["prefix"] = jnp.concatenate([item["trans"], item["add"]], axis=1)
            else:
                prefix = items[g * blocks + n - 1]["prefix"]
                joined = mm(jnp.concatenate([item["reach"], item["trans"]], axis=0), prefix)
                map_ref[rows, lanes] = joined[:GROUP, :DK]
                out_ref[rows, lanes] = item["local"] + joined[:GROUP, DK:]
                item["prefix"] = jnp.concatenate(
                    [joined[GROUP:, :DK], joined[GROUP:, DK:] + item["add"]], axis=1)
            if n == blocks - 1:
                pair_ref[g, :DK, :] = item["prefix"]
    first = seg_ref[:, 0:1].astype(F32)
    last = seg_ref[:, blocks * GROUP - 1 :].astype(F32)
    ends = jnp.where(iota((8, 2 * DK), 0) == 0, first, last)
    for g in range(heads_step):
        pair_ref[g, DK:, :] = ends


def local_stage(queries, keys, values, betas, log_decay, segment):
    tok, heads = queries.shape[0], betas.shape[1]
    blocks = tok // GROUP
    step = 1
    body = lambda *refs: local_kernel(step, blocks, *refs)
    return pl.pallas_call(
        body,
        grid=(heads // step,),
        in_specs=[
            pl.BlockSpec((tok, step * DK), lambda h: (0, h)),
            pl.BlockSpec((tok, 2, step * DK), lambda h: (0, 0, h)),
            pl.BlockSpec((tok, 2, step * DV), lambda h: (0, 0, h)),
            pl.BlockSpec((2, heads, tok), lambda h: (0, 0, 0)),
            pl.BlockSpec((heads, tok), lambda h: (0, 0)),
            pl.BlockSpec((1, tok), lambda h: (0, 0)),
        ],
        out_specs=[
            pl.BlockSpec((step, DK + 8, DK + DV), lambda h: (h, 0, 0)),
            pl.BlockSpec((tok, step * DV), lambda h: (0, h)),
            pl.BlockSpec((tok, step * DK), lambda h: (0, h)),
        ],
        out_shape=[
            jax.ShapeDtypeStruct((heads, DK + 8, DK + DV), F32),
            jax.ShapeDtypeStruct((tok, heads * DV), F32),
            jax.ShapeDtypeStruct((tok, heads * DK), F32),
        ],
        scratch_shapes=[pltpu.VMEM((heads, 8 * blocks, ROWS), F32)],
        compiler_params=pltpu.CompilerParams(dimension_semantics=("arbitrary",)),
        name="local_stage",
    )(queries, keys, values, betas, log_decay, segment.reshape(1, tok))


def prefix_kernel(in_ref, ex_ref, end_ref):
    count = in_ref.shape[0]
    flags = [jnp.where(in_ref[i, DK : DK + 1, :] == in_ref[i - 1, DK + 1 : DK + 2, :], 1.0, 0.0)
             for i in range(1, count)]
    maps = [in_ref[i, :DK, :DK] * (1.0 if i == 0 else flags[i - 1][:, :DK]) for i in range(count)]
    adds = [in_ref[i, :DK, DK:] for i in range(count)]
    width = 1
    while width < count:
        new_maps, new_adds = list(maps), list(adds)
        for i in range(count):
            if i & width:
                j = (i // width) * width - 1
                joined = mm(maps[i], jnp.concatenate([maps[j], adds[j]], axis=1))
                new_maps[i] = joined[:, :DK]
                new_adds[i] = joined[:, DK:] + adds[i]
        maps, adds = new_maps, new_adds
        width *= 2
    r, c = iota((DK, DK), 0), iota((DK, DK), 1)
    ex_ref[0, :, :DK] = (r == c).astype(F32)
    ex_ref[0, :, DK:] = jnp.zeros((DK, DV), F32)
    for i in range(1, count):
        ex_ref[i, :, :DK] = maps[i - 1] * flags[i - 1][:, :DK]
        ex_ref[i, :, DK:] = adds[i - 1] * flags[i - 1][:, DK:]
    end_ref[:DK, :] = adds[count - 1]
    end_ref[DK:, :] = in_ref[count - 1, DK:, :DV]


def incoming_kernel(in_ref, ex_ref, end_ref, out_ref):
    flag = jnp.where(in_ref[0, DK : DK + 1, :DV] == end_ref[DK + 1 : DK + 2, :], 1.0, 0.0)
    state = end_ref[:DK, :] * flag
    for i in range(ex_ref.shape[0]):
        out_ref[i] = mm(ex_ref[i, :, :DK], state) + ex_ref[i, :, DK:]


def far_kernel(pick_ref, local_ref, map_ref, state_ref, gain_ref, weight_ref, normed_ref, up_ref, down_ref):
    heads = state_ref.shape[0]
    for h in range(heads):
        lanes = slice(h * DV, (h + 1) * DV)
        attended = local_ref[:, lanes] + mm(map_ref[:, lanes], state_ref[h])
        mean = jnp.mean(attended * attended, axis=1, keepdims=True)
        normed_ref[:, lanes] = (attended * lax.rsqrt(mean + EPS) * gain_ref[:, lanes]).astype(BF16)
    half = up_ref.shape[0]
    up_ref[...] = dotf(normed_ref[:half, :], weight_ref[...])
    down_ref[...] = dotf(normed_ref[half:, :], weight_ref[...])


def tile_kernel(pick_ref, normed_ref, weight_ref, top_ref, bottom_ref):
    half = top_ref.shape[0]
    top_ref[...] = dotf(normed_ref[:half, :], weight_ref[...])
    bottom_ref[...] = dotf(normed_ref[half:, :], weight_ref[...])


def whole(*shape):
    return pl.BlockSpec(shape, lambda i, *_: (0,) * len(shape))


def far_tile(place, local, mapped, state, gain, weight, width):
    tok, feats = local.shape
    heads = state.shape[0]
    part = jax.ShapeDtypeStruct((tok // 2, width), F32)
    return pl.pallas_call(
        far_kernel,
        grid_spec=pltpu.PrefetchScalarGridSpec(
            num_scalar_prefetch=1, grid=(1,),
            in_specs=[whole(tok, feats), whole(tok, feats), whole(heads, DK, DV), whole(1, feats),
                      pl.BlockSpec((feats, width), lambda i, at: (0, at[0]))],
            out_specs=[whole(tok, feats), whole(tok // 2, width), whole(tok // 2, width)]),
        out_shape=[jax.ShapeDtypeStruct((tok, feats), BF16), part, part],
        name="far_tile",
    )(place, local, mapped, state, gain.reshape(1, feats), weight)


def one_tile(place, normed, weight, width, name):
    tok, feats = normed.shape
    part = jax.ShapeDtypeStruct((tok // 2, width), F32)
    cols = width // 2
    out = pl.BlockSpec((tok // 2, cols), lambda i, at: (0, i))
    return pl.pallas_call(
        tile_kernel,
        grid_spec=pltpu.PrefetchScalarGridSpec(
            num_scalar_prefetch=1, grid=(2,),
            in_specs=[whole(tok, feats), pl.BlockSpec((feats, cols), lambda i, at: (0, 2 * at[0] + i))],
            out_specs=[out, out]),
        out_shape=[part, part],
        name=name,
    )(place, normed, weight)


def summed_output(local, mapped, states, gain, out_weight):
    count = lax.axis_size("head")
    assert count == 4
    mine = lax.axis_index("head")
    width = out_weight.shape[1] // count
    rise = [(i, (i + 1) % count) for i in range(count)]
    fall = [(i, (i - 1) % count) for i in range(count)]
    at = lambda step: ((mine + step) % count).astype(jnp.int32).reshape(1)
    up = lambda x: lax.ppermute(x, "head", rise)
    down = lambda x: lax.ppermute(x, "head", fall)
    normed, far_top, far_bottom = far_tile(at(2), local, mapped, states, gain, out_weight, width)
    got_top, got_bottom = up(far_top), down(far_bottom)
    next_top, next_bottom = one_tile(at(1), normed, out_weight, width, "next_tile")
    last_top, last_bottom = one_tile(at(3), normed, out_weight, width, "last_tile")
    side_bottom, side_top = up(next_bottom), down(last_top)
    got_top, got_bottom = up(next_top + got_top), down(last_bottom + got_bottom)
    own_top, own_bottom = one_tile(at(0), normed, out_weight, width, "own_tile")
    return jnp.concatenate([(own_top + side_top + got_top).astype(BF16),
                            (own_bottom + side_bottom + got_bottom).astype(BF16)], axis=0)


def shards(queries, keys, values, betas, log_decay, segment, gain, out_weight):
    tok, heads = queries.shape[0], betas.shape[1]
    devices = lax.axis_size("ctx")
    span = DOCUMENT_LIMIT // tok
    assert span == heads and devices % span == 0
    groups = [list(range(i, i + span)) for i in range(0, devices, span)]
    pair, local, mapped = local_stage(queries, keys, values, betas, log_decay, segment)
    mine = lax.all_to_all(pair, "ctx", 0, 0, axis_index_groups=groups)
    exclusive, end = pl.pallas_call(
        prefix_kernel,
        out_shape=[jax.ShapeDtypeStruct((span, DK, DK + DV), F32),
                   jax.ShapeDtypeStruct((DK + 8, DV), F32)],
        name="prefix_stage",
    )(mine)
    end = lax.ppermute(end, "ctx", [(i, i + span) for i in range(devices - span)])
    states = pl.pallas_call(
        incoming_kernel,
        out_shape=jax.ShapeDtypeStruct((span, DK, DV), F32),
        name="incoming_stage",
    )(mine, exclusive, end)
    states = lax.all_to_all(states, "ctx", 0, 0, axis_index_groups=groups)
    return summed_output(local, mapped, states, gain, out_weight)


def solution(mesh):
    return jax.shard_map(
        shards,
        mesh=mesh,
        in_specs=(
            P("ctx", "head"),
            P("ctx", None, "head"),
            P("ctx", None, "head"),
            P(None, "head", "ctx"),
            P("head", "ctx"),
            P("ctx"),
            P("head"),
            P("head", None),
        ),
        out_specs=P("ctx", "head"),
        check_vma=False,
    )
```

```python
import jax
import jax.numpy as jnp
from jax import lax
from jax.experimental import pallas as pl
from jax.experimental.pallas import tpu as pltpu
from jax.sharding import PartitionSpec as P

DK = 128
DV = 128
GROUP = 64
ROWS = 2 * GROUP
DOCUMENT_LIMIT = 2048
EPS = 1e-06
F32 = jnp.float32
BF16 = jnp.bfloat16


def dotf(a, b, dims=(((1,), (0,)), ((), ()))):
    return lax.dot_general(a, b, dims, preferred_element_type=F32)


def halves(x):
    hi = x.astype(BF16)
    lo = (x - hi.astype(F32)).astype(BF16)
    return hi, lo


def side(x):
    return jnp.concatenate(halves(x), axis=1)


def mm(a, b):
    left = side(a)
    outs = []
    for c in range(0, b.shape[1], 128):
        right = side(b[:, c : c + 128])
        r = dotf(left, jnp.concatenate([right, right], axis=0))
        outs.append(r[:, :128] + r[:, 128:])
    return outs[0] if len(outs) == 1 else jnp.concatenate(outs, axis=1)


def mm_exact_right(a, b16):
    return dotf(side(a), jnp.concatenate([b16, b16], axis=0))


def iota(shape, dim):
    return lax.broadcasted_iota(jnp.int32, shape, dim)


def invert(systems):
    r, c = iota((ROWS, ROWS), 0), iota((ROWS, ROWS), 1)
    eye = (r == c).astype(F32)
    pair = (r >> 1) == (c >> 1)
    xs = [eye - jnp.where(pair, s, 0.0) for s in systems]
    shift = 1
    while (1 << shift) < ROWS:
        band = ((r >> (shift + 1)) == (c >> (shift + 1))) & ((r >> shift) != (c >> shift))
        if shift < 3:
            ys = [mm(jnp.where(band, s, 0.0), x) for s, x in zip(systems, xs)]
            xs = [x - mm(x, y) for x, y in zip(xs, ys)]
        else:
            size = 1 << shift
            low = lambda m: jnp.concatenate(
                [m[i : i + size] for i in range(size, ROWS, 2 * size)], axis=0)

            def spread(m, rest):
                parts = []
                for i in range(ROWS // (2 * size)):
                    parts += [rest(i), m[i * size : (i + 1) * size]]
                return jnp.concatenate(parts, axis=0)

            empty = jnp.zeros((size, ROWS), F32)
            low_band = low(band.astype(F32))
            ys = [mm(low(s) * low_band, x) for s, x in zip(systems, xs)]
            ys = [spread(y, lambda i: empty) for y in ys]
            lows = [low(x) for x in xs]
            lows = [x - mm(x, y) for x, y in zip(lows, ys)]
            xs = [spread(y, lambda i: x[2 * i * size : (2 * i + 1) * size])
                  for x, y in zip(xs, lows)]
        shift += 1
    return xs


def key_kernel(heads_step, blocks, k_ref, v_ref, beta_ref, log_ref, seg_ref,
               pair_ref, solved_ref, prefix_ref, tab_ref):
    step = pl.program_id(0)
    heads = log_ref.shape[0]

    @pl.when(step == 0)
    def _():
        t, s = iota((GROUP, ROWS), 0), iota((GROUP, ROWS), 1)
        even = (s == 2 * t).astype(F32)
        odd = (s == 2 * t + 1).astype(F32)
        upto = (t <= (s >> 1)).astype(F32)
        flat = (t <= s).astype(F32)
        same = (s == t).astype(F32)
        both = even + odd

        def pick(x, sel):
            return lax.dot_general(x, sel, (((1,), (0,)), ((), ())),
                                   precision=lax.Precision.HIGHEST, preferred_element_type=F32)

        seg = jnp.broadcast_to(seg_ref[...].astype(F32), (heads, blocks * GROUP))
        for n in range(blocks):
            cut = slice(n * GROUP, (n + 1) * GROUP)
            lg = log_ref[:, cut]
            tab_ref[:, 8 * n, :] = pick(lg, upto)
            tab_ref[:, 8 * n + 1, :] = pick(beta_ref[0, :, cut], even) + pick(beta_ref[1, :, cut], odd)
            tab_ref[:, 8 * n + 2, :] = pick(seg[:, cut], both)
            tab_ref[:, 8 * n + 3, :] = pick(lg, flat)
            tab_ref[:, 8 * n + 4, :] = pick(seg[:, cut], same)
            for z in range(5, 8):
                tab_ref[:, 8 * n + z, :] = jnp.zeros((heads, ROWS), F32)

    r, c = iota((ROWS, ROWS), 0), iota((ROWS, ROWS), 1)
    diag = r == c
    eye = diag.astype(F32)
    strictly = r > c

    items = []
    for g in range(heads_step):
        lanes = slice(g * DK, (g + 1) * DK)
        table = tab_ref[step * heads_step + g]
        columns = columns_of(table, blocks)
        prior = table[2:3, 0:1]
        for n in range(blocks):
            key = k_ref[n * GROUP : (n + 1) * GROUP, :, lanes].reshape(ROWS, DK)
            value = v_ref[n * GROUP : (n + 1) * GROUP, :, lanes].reshape(ROWS, DV)
            cum_row, beta_row, seg_row = (table[8 * n + i : 8 * n + i + 1] for i in range(3))
            cum_col, beta_col, seg_col = (columns[:, 8 * n + i : 8 * n + i + 1] for i in range(3))
            cum_last, seg_last = cum_row[:, ROWS - 1 :], seg_row[:, ROWS - 1 :]
            raw = dotf(key, key, (((1,), (1,)), ((), ())))
            own = jnp.where(diag, raw, 0.0)
            rk_row = lax.rsqrt(jnp.sum(own, axis=0, keepdims=True) + EPS)
            rk_col = lax.rsqrt(jnp.sum(own, axis=1, keepdims=True) + EPS)
            tab_ref[step * heads_step + g, 8 * n + 5 : 8 * n + 6, :] = rk_row
            system = jnp.where(strictly & (seg_col == seg_row), raw, 0.0) * (
                beta_col * rk_col * jnp.exp(cum_col)) * (rk_row * jnp.exp(-cum_row))
            entry_row = jnp.where(seg_row == prior, jnp.exp(cum_row), 0.0)
            tail_col = jnp.where(seg_col == seg_last, jnp.exp(cum_last - cum_col), 0.0) * rk_col
            tail_entry = jnp.where(seg_last == prior, jnp.exp(cum_last), 0.0)
            items.append(dict(
                g=g, n=n, key=key, value=value, system=system, wv=beta_row,
                wk=beta_row * rk_row * entry_row, tail=tail_col, tail_entry=tail_entry))
            prior = seg_last

    for item, x in zip(items, invert([item["system"] for item in items])):
        item["pseudo"] = mm_exact_right(x * item["wv"], item["value"])
        item["key_mix"] = mm_exact_right(x * item["wk"], item["key"])
    for item in items:
        g, n = item["g"], item["n"]
        both = jnp.concatenate([item["key_mix"], item["pseudo"]], axis=1)
        solved_ref[g, n] = side(both)
        r2 = dotf(item["key"], side(both * item["tail"]), (((0,), (0,)), ((), ())))
        r2 = r2[:, : 2 * DK] + r2[:, 2 * DK :]
        item["pair"] = (item["tail_entry"] * eye - r2[:, :DK], r2[:, DK:])

    def after(later, earlier):
        joined = mm(later[0], jnp.concatenate(earlier, axis=1))
        return joined[:, :DK], joined[:, DK:] + later[1]

    totals = [[items[g * blocks + n]["pair"] for n in range(blocks)] for g in range(heads_step)]
    first, halfway, third = [t[0] for t in totals], [], []
    halfway = [after(t[1], t[0]) for t in totals]
    upper = [after(t[3], t[2]) for t in totals]
    third = [after(t[2], h) for t, h in zip(totals, halfway)]
    final = [after(u, h) for u, h in zip(upper, halfway)]
    begin = seg_ref[:, 0:1].astype(F32)
    last = seg_ref[:, blocks * GROUP - 1 :].astype(F32)
    ends = jnp.where(iota((8, 2 * DK), 0) == 0, begin, last)
    for g in range(heads_step):
        for n, pair in enumerate((first[g], halfway[g], third[g])):
            prefix_ref[g, n] = side(jnp.concatenate(pair, axis=1))
        pair_ref[g, :DK, :DK] = final[g][0]
        pair_ref[g, :DK, DK:] = final[g][1]
        pair_ref[g, DK:, :] = ends


def columns_of(table, blocks):
    return jnp.concatenate([table, jnp.zeros((ROWS - 8 * blocks, ROWS), F32)], axis=0).T


def mm_sided(a, right):
    width = right.shape[1] // 2
    r = dotf(side(a), jnp.concatenate([right, right], axis=0))
    return r[:, :width] + r[:, width:]


def query_kernel(heads_step, blocks, q_ref, k_ref, solved_ref, prefix_ref, tab_ref, out_ref, map_ref):
    qr, qc = iota((GROUP, ROWS), 0), iota((GROUP, ROWS), 1)
    seen = qc <= 2 * qr + 1
    items = []
    for g in range(heads_step):
        lanes = slice(g * DK, (g + 1) * DK)
        table = tab_ref[g]
        columns = columns_of(table, blocks)
        prior = table[2:3, 0:1]
        for n in range(blocks):
            key = k_ref[n * GROUP : (n + 1) * GROUP, :, lanes].reshape(ROWS, DK)
            query = q_ref[n * GROUP : (n + 1) * GROUP, lanes]
            cum_row, seg_row, rk_row = (table[8 * n + i : 8 * n + i + 1] for i in (0, 2, 5))
            cum_q, seg_q = (columns[:GROUP, 8 * n + i : 8 * n + i + 1] for i in (3, 4))
            raw = dotf(query, key, (((1,), (1,)), ((), ())))
            query32 = query.astype(F32)
            rq = lax.rsqrt(jnp.sum(query32 * query32, axis=1, keepdims=True) + EPS)
            scores = jnp.where(seen & (seg_q == seg_row), raw, 0.0) * (rq * jnp.exp(cum_q)) * (
                rk_row * jnp.exp(-cum_row))
            entry_q = jnp.where(seg_q == prior, jnp.exp(cum_q), 0.0)
            items.append((g, n, query32 * (rq * entry_q), mm_sided(scores, solved_ref[g, n])))
            prior = seg_row[:, ROWS - 1 :]
    for g, n, entering, inner in items:
        rows = slice(n * GROUP, (n + 1) * GROUP)
        lanes = slice(g * DV, (g + 1) * DV)
        reach, local = entering - inner[:, :DK], inner[:, DK:]
        if n:
            joined = mm_sided(reach, prefix_ref[g, n - 1])
            reach, local = joined[:, :DK], local + joined[:, DK:]
        map_ref[rows, lanes] = reach
        out_ref[rows, lanes] = local


KEY_STEP = 2
QUERY_STEP = 2


def key_stage(keys, values, betas, log_decay, segment, step=None):
    tok, heads = keys.shape[0], betas.shape[1]
    blocks = tok // GROUP
    assert blocks == 4
    step = step or KEY_STEP
    body = lambda *refs: key_kernel(step, blocks, *refs)
    return pl.pallas_call(
        body,
        grid=(heads // step,),
        in_specs=[
            pl.BlockSpec((tok, 2, step * DK), lambda h: (0, 0, h)),
            pl.BlockSpec((tok, 2, step * DV), lambda h: (0, 0, h)),
            pl.BlockSpec((2, heads, tok), lambda h: (0, 0, 0)),
            pl.BlockSpec((heads, tok), lambda h: (0, 0)),
            pl.BlockSpec((1, tok), lambda h: (0, 0)),
        ],
        out_specs=[
            pl.BlockSpec((step, DK + 8, DK + DV), lambda h: (h, 0, 0)),
            pl.BlockSpec((step, blocks, ROWS, 2 * (DK + DV)), lambda h: (h, 0, 0, 0)),
            pl.BlockSpec((step, blocks - 1, DK, 2 * (DK + DV)), lambda h: (h, 0, 0, 0)),
            pl.BlockSpec((heads, 8 * blocks, ROWS), lambda h: (0, 0, 0)),
        ],
        out_shape=[
            jax.ShapeDtypeStruct((heads, DK + 8, DK + DV), F32),
            jax.ShapeDtypeStruct((heads, blocks, ROWS, 2 * (DK + DV)), BF16),
            jax.ShapeDtypeStruct((heads, blocks - 1, DK, 2 * (DK + DV)), BF16),
            jax.ShapeDtypeStruct((heads, 8 * blocks, ROWS), F32),
        ],
        compiler_params=pltpu.CompilerParams(dimension_semantics=("arbitrary",)),
        name="key_stage",
    )(keys, values, betas, log_decay, segment.reshape(1, tok))


def query_stage(queries, keys, solved, prefix, table, step=None):
    tok = queries.shape[0]
    heads, blocks = solved.shape[:2]
    step = step or QUERY_STEP
    body = lambda *refs: query_kernel(step, blocks, *refs)
    return pl.pallas_call(
        body,
        grid=(heads // step,),
        in_specs=[
            pl.BlockSpec((tok, step * DK), lambda h: (0, h)),
            pl.BlockSpec((tok, 2, step * DK), lambda h: (0, 0, h)),
            pl.BlockSpec((step, blocks, ROWS, 2 * (DK + DV)), lambda h: (h, 0, 0, 0)),
            pl.BlockSpec((step, blocks - 1, DK, 2 * (DK + DV)), lambda h: (h, 0, 0, 0)),
            pl.BlockSpec((step, 8 * blocks, ROWS), lambda h: (h, 0, 0)),
        ],
        out_specs=[
            pl.BlockSpec((tok, step * DV), lambda h: (0, h)),
            pl.BlockSpec((tok, step * DK), lambda h: (0, h)),
        ],
        out_shape=[
            jax.ShapeDtypeStruct((tok, heads * DV), F32),
            jax.ShapeDtypeStruct((tok, heads * DK), F32),
        ],
        compiler_params=pltpu.CompilerParams(dimension_semantics=("arbitrary",)),
        name="query_stage",
    )(queries, keys, solved, prefix, table)


def prefix_kernel(in_ref, ex_ref, end_ref):
    count = in_ref.shape[0]
    flags = [jnp.where(in_ref[i, DK : DK + 1, :] == in_ref[i - 1, DK + 1 : DK + 2, :], 1.0, 0.0)
             for i in range(1, count)]
    maps = [in_ref[i, :DK, :DK] * (1.0 if i == 0 else flags[i - 1][:, :DK]) for i in range(count)]
    adds = [in_ref[i, :DK, DK:] for i in range(count)]
    width = 1
    while width < count:
        new_maps, new_adds = list(maps), list(adds)
        for i in range(count):
            if i & width:
                j = (i // width) * width - 1
                joined = mm(maps[i], jnp.concatenate([maps[j], adds[j]], axis=1))
                new_maps[i] = joined[:, :DK]
                new_adds[i] = joined[:, DK:] + adds[i]
        maps, adds = new_maps, new_adds
        width *= 2
    r, c = iota((DK, DK), 0), iota((DK, DK), 1)
    ex_ref[0, :, :DK] = (r == c).astype(F32)
    ex_ref[0, :, DK:] = jnp.zeros((DK, DV), F32)
    for i in range(1, count):
        ex_ref[i, :, :DK] = maps[i - 1] * flags[i - 1][:, :DK]
        ex_ref[i, :, DK:] = adds[i - 1] * flags[i - 1][:, DK:]
    end_ref[:DK, :] = adds[count - 1]
    end_ref[DK:, :] = in_ref[count - 1, DK:, :DV]


def incoming_kernel(in_ref, ex_ref, end_ref, out_ref):
    flag = jnp.where(in_ref[0, DK : DK + 1, :DV] == end_ref[DK + 1 : DK + 2, :], 1.0, 0.0)
    state = end_ref[:DK, :] * flag
    for i in range(ex_ref.shape[0]):
        out_ref[i] = mm(ex_ref[i, :, :DK], state) + ex_ref[i, :, DK:]


def far_kernel(pick_ref, local_ref, map_ref, state_ref, gain_ref, weight_ref, normed_ref, up_ref, down_ref):
    heads = state_ref.shape[0]
    for h in range(heads):
        lanes = slice(h * DV, (h + 1) * DV)
        attended = local_ref[:, lanes] + mm(map_ref[:, lanes], state_ref[h])
        mean = jnp.mean(attended * attended, axis=1, keepdims=True)
        normed_ref[:, lanes] = (attended * lax.rsqrt(mean + EPS) * gain_ref[:, lanes]).astype(BF16)
    half = up_ref.shape[0]
    up_ref[...] = dotf(normed_ref[:half, :], weight_ref[...])
    down_ref[...] = dotf(normed_ref[half:, :], weight_ref[...])


def tile_kernel(pick_ref, normed_ref, weight_ref, top_ref, bottom_ref):
    half = top_ref.shape[0]
    top_ref[...] = dotf(normed_ref[:half, :], weight_ref[...])
    bottom_ref[...] = dotf(normed_ref[half:, :], weight_ref[...])


def whole(*shape):
    return pl.BlockSpec(shape, lambda i, *_: (0,) * len(shape))


def far_tile(place, local, mapped, state, gain, weight, width):
    tok, feats = local.shape
    heads = state.shape[0]
    part = jax.ShapeDtypeStruct((tok // 2, width), F32)
    return pl.pallas_call(
        far_kernel,
        grid_spec=pltpu.PrefetchScalarGridSpec(
            num_scalar_prefetch=1, grid=(1,),
            in_specs=[whole(tok, feats), whole(tok, feats), whole(heads, DK, DV), whole(1, feats),
                      pl.BlockSpec((feats, width), lambda i, at: (0, at[0]))],
            out_specs=[whole(tok, feats), whole(tok // 2, width), whole(tok // 2, width)]),
        out_shape=[jax.ShapeDtypeStruct((tok, feats), BF16), part, part],
        name="far_tile",
    )(place, local, mapped, state, gain.reshape(1, feats), weight)


def one_tile(place, normed, weight, width, name):
    tok, feats = normed.shape
    part = jax.ShapeDtypeStruct((tok // 2, width), F32)
    cols = width // 2
    out = pl.BlockSpec((tok // 2, cols), lambda i, at: (0, i))
    return pl.pallas_call(
        tile_kernel,
        grid_spec=pltpu.PrefetchScalarGridSpec(
            num_scalar_prefetch=1, grid=(2,),
            in_specs=[whole(tok, feats), pl.BlockSpec((feats, cols), lambda i, at: (0, 2 * at[0] + i))],
            out_specs=[out, out]),
        out_shape=[part, part],
        name=name,
    )(place, normed, weight)


def sides_kernel(pick_ref, normed_ref, next_w_ref, last_w_ref, nb_ref, lt_ref, nt_ref, lb_ref):
    half = nb_ref.shape[0]
    top, bottom = normed_ref[:half, :], normed_ref[half:, :]
    nb_ref[...] = dotf(bottom, next_w_ref[...])
    lt_ref[...] = dotf(top, last_w_ref[...])
    nt_ref[...] = dotf(top, next_w_ref[...])
    lb_ref[...] = dotf(bottom, last_w_ref[...])


def side_tiles(places, normed, weight, width):
    tok, feats = normed.shape
    steps = 4
    cols = width // steps
    part = jax.ShapeDtypeStruct((tok // 2, width), F32)
    out = pl.BlockSpec((tok // 2, cols), lambda i, at: (0, i))
    return pl.pallas_call(
        sides_kernel,
        grid_spec=pltpu.PrefetchScalarGridSpec(
            num_scalar_prefetch=1, grid=(steps,),
            in_specs=[whole(tok, feats),
                      pl.BlockSpec((feats, cols), lambda i, at: (0, steps * at[0] + i)),
                      pl.BlockSpec((feats, cols), lambda i, at: (0, steps * at[1] + i))],
            out_specs=[out] * 4),
        out_shape=[part] * 4,
        name="side_tiles",
    )(places, normed, weight, weight)


def summed_output(local, mapped, states, gain, out_weight):
    count = lax.axis_size("head")
    assert count == 4
    mine = lax.axis_index("head")
    width = out_weight.shape[1] // count
    rise = [(i, (i + 1) % count) for i in range(count)]
    fall = [(i, (i - 1) % count) for i in range(count)]
    at = lambda step: ((mine + step) & (count - 1)).astype(jnp.int32).reshape(1)
    up = lambda x: lax.ppermute(x, "head", rise)
    down = lambda x: lax.ppermute(x, "head", fall)
    normed, far_top, far_bottom = far_tile(at(2), local, mapped, states, gain, out_weight, width)
    got_top, got_bottom = up(far_top), down(far_bottom)
    next_bottom, last_top, next_top, last_bottom = side_tiles(
        jnp.concatenate([at(1), at(3)]), normed, out_weight, width)
    side_bottom, side_top = up(next_bottom), down(last_top)
    got_top, got_bottom = up(next_top + got_top), down(last_bottom + got_bottom)
    own_top, own_bottom = one_tile(at(0), normed, out_weight, width, "own_tile")
    return jnp.concatenate([(own_top + side_top + got_top).astype(BF16),
                            (own_bottom + side_bottom + got_bottom).astype(BF16)], axis=0)


def shards(queries, keys, values, betas, log_decay, segment, gain, out_weight):
    tok, heads = queries.shape[0], betas.shape[1]
    devices = lax.axis_size("ctx")
    span = DOCUMENT_LIMIT // tok
    assert span == heads and devices % span == 0
    groups = [list(range(i, i + span)) for i in range(0, devices, span)]
    vmem = pl.BlockSpec(memory_space=pltpu.VMEM)
    pair, solved, prefix, table = key_stage(keys, values, betas, log_decay, segment)
    local, mapped = query_stage(queries, keys, solved, prefix, table)
    mine = lax.all_to_all(pair, "ctx", 0, 0, axis_index_groups=groups)
    mine, local, mapped = lax.optimization_barrier((mine, local, mapped))
    exclusive, end = pl.pallas_call(
        prefix_kernel,
        in_specs=[vmem],
        out_specs=[vmem, vmem],
        out_shape=[jax.ShapeDtypeStruct((span, DK, DK + DV), F32),
                   jax.ShapeDtypeStruct((DK + 8, DV), F32)],
        name="prefix_stage",
    )(mine)
    end = lax.ppermute(end, "ctx", [(i, i + span) for i in range(devices - span)])
    states = pl.pallas_call(
        incoming_kernel,
        in_specs=[vmem, vmem, vmem],
        out_specs=vmem,
        out_shape=jax.ShapeDtypeStruct((span, DK, DV), F32),
        name="incoming_stage",
    )(mine, exclusive, end)
    states = lax.all_to_all(states, "ctx", 0, 0, axis_index_groups=groups)
    return summed_output(local, mapped, states, gain, out_weight)


def solution(mesh):
    return jax.shard_map(
        shards,
        mesh=mesh,
        in_specs=(
            P("ctx", "head"),
            P("ctx", None, "head"),
            P("ctx", None, "head"),
            P(None, "head", "ctx"),
            P("head", "ctx"),
            P("ctx"),
            P("head"),
            P("head", None),
        ),
        out_specs=P("ctx", "head"),
        check_vma=False,
    )
```

```python
import jax
import jax.numpy as jnp
from jax import lax
from jax.experimental import pallas as pl
from jax.experimental.pallas import tpu as pltpu
from jax.sharding import PartitionSpec as P


DK = 128
DV = 128
GROUP = 64
ROWS = 2 * GROUP
DOCUMENT_LIMIT = 2048
EPS = 1e-06
F32 = jnp.float32
BF16 = jnp.bfloat16


def dotf(a, b, dims=(((1,), (0,)), ((), ()))):
    return lax.dot_general(a, b, dims, preferred_element_type=F32)


def halves(x):
    hi = x.astype(BF16)
    lo = (x - hi.astype(F32)).astype(BF16)
    return hi, lo


def side(x):
    return jnp.concatenate(halves(x), axis=1)


def mm(a, b):
    left = side(a)
    outs = []
    for c in range(0, b.shape[1], 128):
        right = side(b[:, c : c + 128])
        r = dotf(left, jnp.concatenate([right, right], axis=0))
        outs.append(r[:, :128] + r[:, 128:])
    return outs[0] if len(outs) == 1 else jnp.concatenate(outs, axis=1)


def mm_exact_right(a, b16):
    return dotf(side(a), jnp.concatenate([b16, b16], axis=0))


def iota(shape, dim):
    return lax.broadcasted_iota(jnp.int32, shape, dim)


def invert(systems):
    r, c = iota((ROWS, ROWS), 0), iota((ROWS, ROWS), 1)
    eye = (r == c).astype(F32)
    pair = (r >> 1) == (c >> 1)
    xs = [eye - jnp.where(pair, s, 0.0) for s in systems]
    shift = 1
    while (1 << shift) < ROWS:
        band = ((r >> (shift + 1)) == (c >> (shift + 1))) & ((r >> shift) != (c >> shift))
        if shift < 3:
            ys = [mm(jnp.where(band, s, 0.0), x) for s, x in zip(systems, xs)]
            xs = [x - mm(x, y) for x, y in zip(xs, ys)]
        else:
            size = 1 << shift
            low = lambda m: jnp.concatenate(
                [m[i : i + size] for i in range(size, ROWS, 2 * size)], axis=0)

            def spread(m, rest):
                parts = []
                for i in range(ROWS // (2 * size)):
                    parts += [rest(i), m[i * size : (i + 1) * size]]
                return jnp.concatenate(parts, axis=0)

            empty = jnp.zeros((size, ROWS), F32)
            low_band = low(band.astype(F32))
            ys = [mm(low(s) * low_band, x) for s, x in zip(systems, xs)]
            ys = [spread(y, lambda i: empty) for y in ys]
            lows = [low(x) for x in xs]
            lows = [x - mm(x, y) for x, y in zip(lows, ys)]
            xs = [spread(y, lambda i: x[2 * i * size : (2 * i + 1) * size])
                  for x, y in zip(xs, lows)]
        shift += 1
    return xs


def key_kernel(heads_step, blocks, k_ref, v_ref, beta_ref, log_ref, seg_ref,
               pair_ref, solved_ref, prefix_ref, tab_ref):
    step = pl.program_id(0)
    heads = log_ref.shape[0]

    @pl.when(step == 0)
    def _():
        t, s = iota((GROUP, ROWS), 0), iota((GROUP, ROWS), 1)
        even = (s == 2 * t).astype(F32)
        odd = (s == 2 * t + 1).astype(F32)
        upto = (t <= (s >> 1)).astype(F32)
        flat = (t <= s).astype(F32)
        same = (s == t).astype(F32)
        both = even + odd

        def pick(x, sel):
            return lax.dot_general(x, sel, (((1,), (0,)), ((), ())),
                                   precision=lax.Precision.HIGHEST, preferred_element_type=F32)

        seg = jnp.broadcast_to(seg_ref[...].astype(F32), (heads, blocks * GROUP))
        for n in range(blocks):
            cut = slice(n * GROUP, (n + 1) * GROUP)
            lg = log_ref[:, cut]
            tab_ref[:, 8 * n, :] = pick(lg, upto)
            tab_ref[:, 8 * n + 1, :] = pick(beta_ref[0, :, cut], even) + pick(beta_ref[1, :, cut], odd)
            tab_ref[:, 8 * n + 2, :] = pick(seg[:, cut], both)
            tab_ref[:, 8 * n + 3, :] = pick(lg, flat)
            tab_ref[:, 8 * n + 4, :] = pick(seg[:, cut], same)
            for z in range(5, 8):
                tab_ref[:, 8 * n + z, :] = jnp.zeros((heads, ROWS), F32)

    r, c = iota((ROWS, ROWS), 0), iota((ROWS, ROWS), 1)
    diag = r == c
    eye = diag.astype(F32)
    strictly = r > c

    items = []
    for g in range(heads_step):
        lanes = slice(g * DK, (g + 1) * DK)
        table = tab_ref[step * heads_step + g]
        columns = columns_of(table, blocks)
        prior = table[2:3, 0:1]
        for n in range(blocks):
            key = k_ref[n * GROUP : (n + 1) * GROUP, :, lanes].reshape(ROWS, DK)
            value = v_ref[n * GROUP : (n + 1) * GROUP, :, lanes].reshape(ROWS, DV)
            cum_row, beta_row, seg_row = (table[8 * n + i : 8 * n + i + 1] for i in range(3))
            cum_col, beta_col, seg_col = (columns[:, 8 * n + i : 8 * n + i + 1] for i in range(3))
            cum_last, seg_last = cum_row[:, ROWS - 1 :], seg_row[:, ROWS - 1 :]
            raw = dotf(key, key, (((1,), (1,)), ((), ())))
            own = jnp.where(diag, raw, 0.0)
            rk_row = lax.rsqrt(jnp.sum(own, axis=0, keepdims=True) + EPS)
            rk_col = lax.rsqrt(jnp.sum(own, axis=1, keepdims=True) + EPS)
            tab_ref[step * heads_step + g, 8 * n + 5 : 8 * n + 6, :] = rk_row
            system = jnp.where(strictly & (seg_col == seg_row), raw, 0.0) * (
                beta_col * rk_col * jnp.exp(cum_col)) * (rk_row * jnp.exp(-cum_row))
            entry_row = jnp.where(seg_row == prior, jnp.exp(cum_row), 0.0)
            tail_col = jnp.where(seg_col == seg_last, jnp.exp(cum_last - cum_col), 0.0) * rk_col
            tail_entry = jnp.where(seg_last == prior, jnp.exp(cum_last), 0.0)
            items.append(dict(
                g=g, n=n, key=key, value=value, system=system, wv=beta_row,
                wk=beta_row * rk_row * entry_row, tail=tail_col, tail_entry=tail_entry))
            prior = seg_last

    for item, x in zip(items, invert([item["system"] for item in items])):
        item["pseudo"] = mm_exact_right(x * item["wv"], item["value"])
        item["key_mix"] = mm_exact_right(x * item["wk"], item["key"])
    for item in items:
        g, n = item["g"], item["n"]
        both = jnp.concatenate([item["key_mix"], item["pseudo"]], axis=1)
        solved_ref[g, n] = side(both)
        r2 = dotf(item["key"], side(both * item["tail"]), (((0,), (0,)), ((), ())))
        r2 = r2[:, : 2 * DK] + r2[:, 2 * DK :]
        item["pair"] = (item["tail_entry"] * eye - r2[:, :DK], r2[:, DK:])

    def after(later, earlier):
        joined = mm(later[0], jnp.concatenate(earlier, axis=1))
        return joined[:, :DK], joined[:, DK:] + later[1]

    totals = [[items[g * blocks + n]["pair"] for n in range(blocks)] for g in range(heads_step)]
    first, halfway, third = [t[0] for t in totals], [], []
    halfway = [after(t[1], t[0]) for t in totals]
    upper = [after(t[3], t[2]) for t in totals]
    third = [after(t[2], h) for t, h in zip(totals, halfway)]
    final = [after(u, h) for u, h in zip(upper, halfway)]
    begin = seg_ref[:, 0:1].astype(F32)
    last = seg_ref[:, blocks * GROUP - 1 :].astype(F32)
    ends = jnp.where(iota((8, 2 * DK), 0) == 0, begin, last)
    for g in range(heads_step):
        for n, pair in enumerate((first[g], halfway[g], third[g])):
            prefix_ref[g, n] = side(jnp.concatenate(pair, axis=1))
        pair_ref[g, :DK, :DK] = final[g][0]
        pair_ref[g, :DK, DK:] = final[g][1]
        pair_ref[g, DK:, :] = ends


def resident():
    return pl.BlockSpec(memory_space=pltpu.VMEM)


def held(x):
    return pltpu.with_memory_space_constraint(x, pltpu.VMEM)


def columns_of(table, blocks):
    return jnp.concatenate([table, jnp.zeros((ROWS - 8 * blocks, ROWS), F32)], axis=0).T


def mm_sided(a, right):
    width = right.shape[1] // 2
    r = dotf(side(a), jnp.concatenate([right, right], axis=0))
    return r[:, :width] + r[:, width:]


def query_kernel(heads_step, blocks, q_ref, k_ref, solved_ref, prefix_ref, tab_ref, out_ref, map_ref):
    qr, qc = iota((GROUP, ROWS), 0), iota((GROUP, ROWS), 1)
    seen = qc <= 2 * qr + 1
    items = []
    for g in range(heads_step):
        lanes = slice(g * DK, (g + 1) * DK)
        table = tab_ref[g]
        columns = columns_of(table, blocks)
        prior = table[2:3, 0:1]
        for n in range(blocks):
            key = k_ref[n * GROUP : (n + 1) * GROUP, :, lanes].reshape(ROWS, DK)
            query = q_ref[n * GROUP : (n + 1) * GROUP, lanes]
            cum_row, seg_row, rk_row = (table[8 * n + i : 8 * n + i + 1] for i in (0, 2, 5))
            cum_q, seg_q = (columns[:GROUP, 8 * n + i : 8 * n + i + 1] for i in (3, 4))
            raw = dotf(query, key, (((1,), (1,)), ((), ())))
            query32 = query.astype(F32)
            rq = lax.rsqrt(jnp.sum(query32 * query32, axis=1, keepdims=True) + EPS)
            scores = jnp.where(seen & (seg_q == seg_row), raw, 0.0) * (rq * jnp.exp(cum_q)) * (
                rk_row * jnp.exp(-cum_row))
            entry_q = jnp.where(seg_q == prior, jnp.exp(cum_q), 0.0)
            items.append((g, n, query32 * (rq * entry_q), mm_sided(scores, solved_ref[g, n])))
            prior = seg_row[:, ROWS - 1 :]
    for g, n, entering, inner in items:
        rows = slice(n * GROUP, (n + 1) * GROUP)
        lanes = slice(g * DV, (g + 1) * DV)
        reach, local = entering - inner[:, :DK], inner[:, DK:]
        if n:
            joined = mm_sided(reach, prefix_ref[g, n - 1])
            reach, local = joined[:, :DK], local + joined[:, DK:]
        map_ref[rows, lanes] = reach
        out_ref[rows, lanes] = local


KEY_STEP = 2
QUERY_STEP = 2


def key_stage(keys, values, betas, log_decay, segment, step=None):
    tok, heads = keys.shape[0], betas.shape[1]
    blocks = tok // GROUP
    assert blocks == 4
    step = step or KEY_STEP
    body = lambda *refs: key_kernel(step, blocks, *refs)
    return pl.pallas_call(
        body,
        grid=(heads // step,),
        in_specs=[
            pl.BlockSpec((tok, 2, step * DK), lambda h: (0, 0, h)),
            pl.BlockSpec((tok, 2, step * DV), lambda h: (0, 0, h)),
            pl.BlockSpec((2, heads, tok), lambda h: (0, 0, 0)),
            pl.BlockSpec((heads, tok), lambda h: (0, 0)),
            pl.BlockSpec((1, tok), lambda h: (0, 0)),
        ],
        out_specs=[
            pl.BlockSpec((step, DK + 8, DK + DV), lambda h: (h, 0, 0)),
            pl.BlockSpec((step, blocks, ROWS, 2 * (DK + DV)), lambda h: (h, 0, 0, 0)),
            pl.BlockSpec((step, blocks - 1, DK, 2 * (DK + DV)), lambda h: (h, 0, 0, 0)),
            pl.BlockSpec((heads, 8 * blocks, ROWS), lambda h: (0, 0, 0)),
        ],
        out_shape=[
            jax.ShapeDtypeStruct((heads, DK + 8, DK + DV), F32),
            jax.ShapeDtypeStruct((heads, blocks, ROWS, 2 * (DK + DV)), BF16),
            jax.ShapeDtypeStruct((heads, blocks - 1, DK, 2 * (DK + DV)), BF16),
            jax.ShapeDtypeStruct((heads, 8 * blocks, ROWS), F32),
        ],
        compiler_params=pltpu.CompilerParams(dimension_semantics=("arbitrary",)),
        name="key_stage",
    )(keys, values, betas, log_decay, segment.reshape(1, tok))


def query_stage(queries, keys, solved, prefix, table, step=None):
    tok = queries.shape[0]
    heads, blocks = solved.shape[:2]
    step = step or QUERY_STEP
    body = lambda *refs: query_kernel(step, blocks, *refs)
    return pl.pallas_call(
        body,
        grid=(heads // step,),
        in_specs=[
            pl.BlockSpec((tok, step * DK), lambda h: (0, h)),
            pl.BlockSpec((tok, 2, step * DK), lambda h: (0, 0, h)),
            pl.BlockSpec((step, blocks, ROWS, 2 * (DK + DV)), lambda h: (h, 0, 0, 0)),
            pl.BlockSpec((step, blocks - 1, DK, 2 * (DK + DV)), lambda h: (h, 0, 0, 0)),
            pl.BlockSpec((step, 8 * blocks, ROWS), lambda h: (h, 0, 0)),
        ],
        out_specs=[
            pl.BlockSpec((tok, step * DV), lambda h: (0, h)),
            pl.BlockSpec((tok, step * DK), lambda h: (0, h)),
        ],
        out_shape=[
            jax.ShapeDtypeStruct((tok, heads * DV), F32),
            jax.ShapeDtypeStruct((tok, heads * DK), F32),
        ],
        compiler_params=pltpu.CompilerParams(dimension_semantics=("arbitrary",)),
        name="query_stage",
    )(queries, keys, solved, prefix, table)


def prefix_kernel(in_ref, ex_ref, end_ref, ends_ref):
    count = in_ref.shape[0]
    flags = [jnp.where(in_ref[i, DK : DK + 1, :] == in_ref[i - 1, DK + 1 : DK + 2, :], 1.0, 0.0)
             for i in range(1, count)]
    maps = [in_ref[i, :DK, :DK] * (1.0 if i == 0 else flags[i - 1][:, :DK]) for i in range(count)]
    adds = [in_ref[i, :DK, DK:] for i in range(count)]
    width = 1
    while width < count:
        new_maps, new_adds = list(maps), list(adds)
        for i in range(count):
            if i & width:
                j = (i // width) * width - 1
                joined = mm(maps[i], jnp.concatenate([maps[j], adds[j]], axis=1))
                new_maps[i] = joined[:, :DK]
                new_adds[i] = joined[:, DK:] + adds[i]
        maps, adds = new_maps, new_adds
        width *= 2
    r, c = iota((DK, DK), 0), iota((DK, DK), 1)
    ex_ref[0, :, :DK] = (r == c).astype(F32)
    ex_ref[0, :, DK:] = jnp.zeros((DK, DV), F32)
    for i in range(1, count):
        ex_ref[i, :, :DK] = maps[i - 1] * flags[i - 1][:, :DK]
        ex_ref[i, :, DK:] = adds[i - 1] * flags[i - 1][:, DK:]
    end_ref[:DK, :] = adds[count - 1]
    end_ref[DK:, :] = in_ref[count - 1, DK:, :DV]
    ends_ref[...] = in_ref[0, DK:, :DV]


def incoming_kernel(ends_ref, ex_ref, end_ref, out_ref):
    flag = jnp.where(ends_ref[0:1, :] == end_ref[DK + 1 : DK + 2, :], 1.0, 0.0)
    state = end_ref[:DK, :] * flag
    for i in range(ex_ref.shape[0]):
        out_ref[i] = mm(ex_ref[i, :, :DK], state) + ex_ref[i, :, DK:]


def far_kernel(pick_ref, local_ref, map_ref, state_ref, gain_ref, weight_ref, normed_ref, up_ref, down_ref):
    heads = state_ref.shape[0]

    @pl.when(pl.program_id(0) == 0)
    def _():
        for h in range(heads):
            lanes = slice(h * DV, (h + 1) * DV)
            attended = local_ref[:, lanes] + mm(map_ref[:, lanes], state_ref[h])
            mean = jnp.mean(attended * attended, axis=1, keepdims=True)
            normed_ref[:, lanes] = (attended * lax.rsqrt(mean + EPS) * gain_ref[:, lanes]).astype(BF16)

    half = up_ref.shape[0]
    up_ref[...] = dotf(normed_ref[:half, :], weight_ref[...])
    down_ref[...] = dotf(normed_ref[half:, :], weight_ref[...])


def tile_kernel(pick_ref, normed_ref, weight_ref, top_ref, bottom_ref):
    half = top_ref.shape[0]
    top_ref[...] = dotf(normed_ref[:half, :], weight_ref[...])
    bottom_ref[...] = dotf(normed_ref[half:, :], weight_ref[...])


def whole(*shape):
    return pl.BlockSpec(shape, lambda i, *_: (0,) * len(shape))


def far_tile(place, local, mapped, state, gain, weight, width):
    tok, feats = local.shape
    part = pltpu.VMEM((tok // 2, width), F32)
    steps = 2
    cols = width // steps
    out = pl.BlockSpec((tok // 2, cols), lambda i, at: (0, i))
    return pl.pallas_call(
        far_kernel,
        grid_spec=pltpu.PrefetchScalarGridSpec(
            num_scalar_prefetch=1, grid=(steps,),
            in_specs=[whole(tok, feats), whole(tok, feats), resident(), whole(1, feats),
                      pl.BlockSpec((feats, cols), lambda i, at: (0, steps * at[0] + i))],
            out_specs=[whole(tok, feats), out, out]),
        out_shape=[jax.ShapeDtypeStruct((tok, feats), BF16), part, part],
        compiler_params=pltpu.CompilerParams(vmem_limit_bytes=57 << 20),
        name="far_tile",
    )(place, local, mapped, held(state), gain.reshape(1, feats), weight)


def join_kernel(nt_ref, gt_ref, lb_ref, gb_ref, top_ref, bottom_ref):
    top_ref[...] = nt_ref[...] + gt_ref[...]
    bottom_ref[...] = lb_ref[...] + gb_ref[...]


def joined(next_top, got_top, last_bottom, got_bottom):
    return pl.pallas_call(
        join_kernel,
        in_specs=[resident()] * 4,
        out_specs=[resident()] * 2,
        out_shape=[pltpu.VMEM(next_top.shape, F32)] * 2,
        compiler_params=pltpu.CompilerParams(vmem_limit_bytes=57 << 20),
        name="join_tiles",
    )(held(next_top), held(got_top), held(last_bottom), held(got_bottom))


def one_tile(place, normed, weight, width):
    tok, feats = normed.shape
    part = pltpu.VMEM((tok // 2, width), F32)
    cols = width // 2
    out = pl.BlockSpec((tok // 2, cols), lambda i, at: (0, i))
    return pl.pallas_call(
        tile_kernel,
        grid_spec=pltpu.PrefetchScalarGridSpec(
            num_scalar_prefetch=1, grid=(2,),
            in_specs=[whole(tok, feats), pl.BlockSpec((feats, cols), lambda i, at: (0, 2 * at[0] + i))],
            out_specs=[out, out]),
        out_shape=[part, part],
        compiler_params=pltpu.CompilerParams(vmem_limit_bytes=57 << 20),
    )(place, normed, weight)


def sides_kernel(pick_ref, normed_ref, next_w_ref, last_w_ref, nb_ref, lt_ref, nt_ref, lb_ref):
    half = nb_ref.shape[0]
    top, bottom = normed_ref[:half, :], normed_ref[half:, :]
    nb_ref[...] = dotf(bottom, next_w_ref[...])
    lt_ref[...] = dotf(top, last_w_ref[...])
    nt_ref[...] = dotf(top, next_w_ref[...])
    lb_ref[...] = dotf(bottom, last_w_ref[...])


def side_tiles(places, normed, weight, width):
    tok, feats = normed.shape
    steps = 4
    cols = width // steps
    part = jax.ShapeDtypeStruct((tok // 2, width), F32)
    out = pl.BlockSpec((tok // 2, cols), lambda i, at: (0, i))
    return pl.pallas_call(
        sides_kernel,
        grid_spec=pltpu.PrefetchScalarGridSpec(
            num_scalar_prefetch=1, grid=(steps,),
            in_specs=[whole(tok, feats),
                      pl.BlockSpec((feats, cols), lambda i, at: (0, steps * at[0] + i)),
                      pl.BlockSpec((feats, cols), lambda i, at: (0, steps * at[1] + i))],
            out_specs=[out] * 4),
        out_shape=[part] * 2 + [pltpu.VMEM((tok // 2, width), F32)] * 2,
        compiler_params=pltpu.CompilerParams(vmem_limit_bytes=57 << 20),
        name="side_tiles",
    )(places, normed, weight, weight)


def finish_kernel(ot_ref, st_ref, gt_ref, ob_ref, sb_ref, gb_ref, out_ref):
    half = ot_ref.shape[0]
    out_ref[:half, :] = (ot_ref[...] + st_ref[...] + gt_ref[...]).astype(BF16)
    out_ref[half:, :] = (ob_ref[...] + sb_ref[...] + gb_ref[...]).astype(BF16)


def summed_output(local, mapped, states, gain, out_weight):
    count = lax.axis_size("head")
    assert count == 4
    mine = lax.axis_index("head")
    width = out_weight.shape[1] // count
    rise = [(i, (i + 1) % count) for i in range(count)]
    fall = [(i, (i - 1) % count) for i in range(count)]
    at = lambda step: ((mine + step) & (count - 1)).astype(jnp.int32).reshape(1)
    up = lambda x: lax.ppermute(x, "head", rise)
    down = lambda x: lax.ppermute(x, "head", fall)
    normed, far_top, far_bottom = far_tile(at(2), local, mapped, states, gain, out_weight, width)
    got_top, got_bottom = up(far_top), down(far_bottom)
    next_bottom, last_top, next_top, last_bottom = side_tiles(
        jnp.concatenate([at(1), at(3)]), normed, out_weight, width)
    side_bottom = up(next_bottom)
    side_top = down(last_top)
    next_top, last_bottom = joined(next_top, got_top, last_bottom, got_bottom)
    got_top, got_bottom = up(next_top), down(last_bottom)
    own_top, own_bottom = one_tile(at(0), normed, out_weight, width)
    return pl.pallas_call(
        finish_kernel,
        in_specs=[resident()] * 6,
        out_shape=jax.ShapeDtypeStruct((2 * own_top.shape[0], width), BF16),
        compiler_params=pltpu.CompilerParams(vmem_limit_bytes=57 << 20),
        name="finish",
    )(*map(held, (own_top, side_top, got_top, own_bottom, side_bottom, got_bottom)))


def shards(queries, keys, values, betas, log_decay, segment, gain, out_weight):
    tok, heads = queries.shape[0], betas.shape[1]
    devices = lax.axis_size("ctx")
    span = DOCUMENT_LIMIT // tok
    assert span == heads and devices % span == 0
    groups = [list(range(i, i + span)) for i in range(0, devices, span)]
    pair, solved, prefix, table = key_stage(keys, values, betas, log_decay, segment)
    local, mapped = query_stage(queries, keys, solved, prefix, table)
    mine = lax.all_to_all(pair, "ctx", 0, 0, axis_index_groups=groups)
    mine, local, mapped = lax.optimization_barrier((mine, local, mapped))
    exclusive, end, ends = pl.pallas_call(
        prefix_kernel,
        in_specs=[resident()],
        out_specs=[resident(), resident(), resident()],
        out_shape=[pltpu.VMEM((span, DK, DK + DV), F32), pltpu.VMEM((DK + 8, DV), F32),
                   pltpu.VMEM((8, DV), F32)],
        compiler_params=pltpu.CompilerParams(vmem_limit_bytes=57 << 20),
        name="prefix_stage",
    )(held(mine))
    end = lax.ppermute(end, "ctx", [(i, i + span) for i in range(devices - span)])
    states = pl.pallas_call(
        incoming_kernel,
        in_specs=[resident(), resident(), resident()],
        out_specs=resident(),
        out_shape=pltpu.VMEM((span, DK, DV), F32),
        compiler_params=pltpu.CompilerParams(vmem_limit_bytes=57 << 20),
        name="incoming_stage",
    )(held(ends), held(exclusive), held(end))
    states = lax.all_to_all(states, "ctx", 0, 0, axis_index_groups=groups)
    return summed_output(local, mapped, states, gain, out_weight)


def solution(mesh):
    return jax.shard_map(
        shards,
        mesh=mesh,
        in_specs=(
            P("ctx", "head"),
            P("ctx", None, "head"),
            P("ctx", None, "head"),
            P(None, "head", "ctx"),
            P("head", "ctx"),
            P("ctx"),
            P("head"),
            P("head", None),
        ),
        out_specs=P("ctx", "head"),
        check_vma=False,
    )
```

```python
import jax
import jax.numpy as jnp
from jax import lax
from jax.experimental import pallas as pl
from jax.experimental.pallas import tpu as pltpu
from jax.sharding import PartitionSpec as P


DK = 128
DV = 128
GROUP = 64
ROWS = 2 * GROUP
DOCUMENT_LIMIT = 2048
EPS = 1e-06
F32 = jnp.float32
BF16 = jnp.bfloat16


def dotf(a, b, dims=(((1,), (0,)), ((), ()))):
    return lax.dot_general(a, b, dims, preferred_element_type=F32)


def halves(x):
    hi = x.astype(BF16)
    lo = (x - hi.astype(F32)).astype(BF16)
    return hi, lo


def side(x):
    return jnp.concatenate(halves(x), axis=1)


def mm(a, b):
    left = side(a)
    outs = []
    for c in range(0, b.shape[1], 128):
        right = side(b[:, c : c + 128])
        r = dotf(left, jnp.concatenate([right, right], axis=0))
        outs.append(r[:, :128] + r[:, 128:])
    return outs[0] if len(outs) == 1 else jnp.concatenate(outs, axis=1)


def mm_tall(a, b):
    m = a.shape[0]
    r = dotf(jnp.concatenate(halves(a), axis=0), side(b))
    return r[:m, :128] + (r[:m, 128:] + r[m:, :128])


def mm_exact_right(a, b16):
    return dotf(side(a), jnp.concatenate([b16, b16], axis=0))


def iota(shape, dim):
    return lax.broadcasted_iota(jnp.int32, shape, dim)


def invert(systems):
    r, c = iota((ROWS, ROWS), 0), iota((ROWS, ROWS), 1)
    eye = (r == c).astype(F32)
    pair = (r >> 1) == (c >> 1)
    xs = [eye - jnp.where(pair, s, 0.0) for s in systems]
    shift = 1
    while (1 << shift) < ROWS:
        band = ((r >> (shift + 1)) == (c >> (shift + 1))) & ((r >> shift) != (c >> shift))
        if shift < 3:
            ys = [mm(jnp.where(band, s, 0.0), x) for s, x in zip(systems, xs)]
            xs = [x - mm(x, y) for x, y in zip(xs, ys)]
        else:
            size = 1 << shift
            low = lambda m: jnp.concatenate(
                [m[i : i + size] for i in range(size, ROWS, 2 * size)], axis=0)

            def spread(m, rest):
                parts = []
                for i in range(ROWS // (2 * size)):
                    parts += [rest(i), m[i * size : (i + 1) * size]]
                return jnp.concatenate(parts, axis=0)

            empty = jnp.zeros((size, ROWS), F32)
            low_band = low(band.astype(F32))
            ys = [mm_tall(low(s) * low_band, x) for s, x in zip(systems, xs)]
            ys = [spread(y, lambda i: empty) for y in ys]
            lows = [low(x) for x in xs]
            lows = [x - mm_tall(x, y) for x, y in zip(lows, ys)]
            xs = [spread(y, lambda i: x[2 * i * size : (2 * i + 1) * size])
                  for x, y in zip(xs, lows)]
        shift += 1
    return xs


def key_kernel(heads_step, blocks, k_ref, v_ref, beta_ref, log_ref, seg_ref,
               pair_ref, solved_ref, prefix_ref, tab_ref):
    step = pl.program_id(0)
    heads = log_ref.shape[0]

    @pl.when(step == 0)
    def _():
        t, s = iota((GROUP, ROWS), 0), iota((GROUP, ROWS), 1)
        even = (s == 2 * t).astype(F32)
        odd = (s == 2 * t + 1).astype(F32)
        upto = (t <= (s >> 1)).astype(F32)
        flat = (t <= s).astype(F32)
        same = (s == t).astype(F32)
        both = even + odd

        def pick(x, sel):
            return lax.dot_general(x, sel, (((1,), (0,)), ((), ())),
                                   precision=lax.Precision.HIGHEST, preferred_element_type=F32)

        def stacked(x):
            return jnp.concatenate([x[:, n * GROUP : (n + 1) * GROUP] for n in range(blocks)], axis=0)

        seg = stacked(jnp.broadcast_to(seg_ref[...].astype(F32), (heads, blocks * GROUP)))
        lg = stacked(log_ref[...])
        kinds = (pick(lg, upto),
                 pick(stacked(beta_ref[0]), even) + pick(stacked(beta_ref[1]), odd),
                 pick(seg, both), pick(lg, flat), pick(seg, same))
        for n in range(blocks):
            for i, kind in enumerate(kinds):
                tab_ref[:, 8 * n + i, :] = kind[n * heads : (n + 1) * heads]
            for z in range(len(kinds), 8):
                tab_ref[:, 8 * n + z, :] = jnp.zeros((heads, ROWS), F32)

    r, c = iota((ROWS, ROWS), 0), iota((ROWS, ROWS), 1)
    diag = r == c
    eye = diag.astype(F32)
    strictly = r > c

    items = []
    for g in range(heads_step):
        lanes = slice(g * DK, (g + 1) * DK)
        table = tab_ref[step * heads_step + g]
        columns = columns_of(table, blocks)
        prior = table[2:3, 0:1]
        for n in range(blocks):
            key = k_ref[n * GROUP : (n + 1) * GROUP, :, lanes].reshape(ROWS, DK)
            value = v_ref[n * GROUP : (n + 1) * GROUP, :, lanes].reshape(ROWS, DV)
            cum_row, beta_row, seg_row = (table[8 * n + i : 8 * n + i + 1] for i in range(3))
            cum_col, beta_col, seg_col = (columns[:, 8 * n + i : 8 * n + i + 1] for i in range(3))
            cum_last, seg_last = cum_row[:, ROWS - 1 :], seg_row[:, ROWS - 1 :]
            raw = dotf(key, key, (((1,), (1,)), ((), ())))
            own = jnp.where(diag, raw, 0.0)
            rk_row = lax.rsqrt(jnp.sum(own, axis=0, keepdims=True) + EPS)
            rk_col = lax.rsqrt(jnp.sum(own, axis=1, keepdims=True) + EPS)
            tab_ref[step * heads_step + g, 8 * n + 5 : 8 * n + 6, :] = rk_row
            system = jnp.where(strictly & (seg_col == seg_row), raw, 0.0) * (
                beta_col * rk_col * jnp.exp(cum_col)) * (rk_row * jnp.exp(-cum_row))
            entry_row = jnp.where(seg_row == prior, jnp.exp(cum_row), 0.0)
            tail_col = jnp.where(seg_col == seg_last, jnp.exp(cum_last - cum_col), 0.0) * rk_col
            tail_entry = jnp.where(seg_last == prior, jnp.exp(cum_last), 0.0)
            items.append(dict(
                g=g, n=n, key=key, value=value, system=system, wv=beta_row,
                wk=beta_row * rk_row * entry_row, tail=tail_col, tail_entry=tail_entry))
            prior = seg_last

    for item, x in zip(items, invert([item["system"] for item in items])):
        item["pseudo"] = mm_exact_right(x * item["wv"], item["value"])
        item["key_mix"] = mm_exact_right(x * item["wk"], item["key"])
    for item in items:
        g, n = item["g"], item["n"]
        both = jnp.concatenate([item["key_mix"], item["pseudo"]], axis=1)
        solved_ref[g, n] = side(both)
        r2 = dotf(item["key"], side(both * item["tail"]), (((0,), (0,)), ((), ())))
        r2 = r2[:, : 2 * DK] + r2[:, 2 * DK :]
        item["pair"] = (item["tail_entry"] * eye - r2[:, :DK], r2[:, DK:])

    def after(later, earlier):
        joined = mm(later[0], jnp.concatenate(earlier, axis=1))
        return joined[:, :DK], joined[:, DK:] + later[1]

    totals = [[items[g * blocks + n]["pair"] for n in range(blocks)] for g in range(heads_step)]
    first, halfway, third = [t[0] for t in totals], [], []
    halfway = [after(t[1], t[0]) for t in totals]
    upper = [after(t[3], t[2]) for t in totals]
    third = [after(t[2], h) for t, h in zip(totals, halfway)]
    final = [after(u, h) for u, h in zip(upper, halfway)]
    begin = seg_ref[:, 0:1].astype(F32)
    last = seg_ref[:, blocks * GROUP - 1 :].astype(F32)
    ends = jnp.where(iota((8, 2 * DK), 0) == 0, begin, last)
    for g in range(heads_step):
        for n, pair in enumerate((first[g], halfway[g], third[g])):
            prefix_ref[g, n] = side(jnp.concatenate(pair, axis=1))
        pair_ref[g, :DK, :DK] = final[g][0]
        pair_ref[g, :DK, DK:] = final[g][1]
        pair_ref[g, DK:, :] = ends


def resident():
    return pl.BlockSpec(memory_space=pltpu.VMEM)


def held(x):
    return pltpu.with_memory_space_constraint(x, pltpu.VMEM)


def columns_of(table, blocks):
    return jnp.concatenate([table, jnp.zeros((ROWS - 8 * blocks, ROWS), F32)], axis=0).T


def mm_sided(a, right):
    width = right.shape[1] // 2
    r = dotf(side(a), jnp.concatenate([right, right], axis=0))
    return r[:, :width] + r[:, width:]


def query_kernel(heads_step, blocks, q_ref, k_ref, solved_ref, prefix_ref, tab_ref, out_ref, map_ref):
    qr, qc = iota((GROUP, ROWS), 0), iota((GROUP, ROWS), 1)
    seen = qc <= 2 * qr + 1
    items = []
    for g in range(heads_step):
        lanes = slice(g * DK, (g + 1) * DK)
        table = tab_ref[g]
        columns = columns_of(table, blocks)
        prior = table[2:3, 0:1]
        for n in range(blocks):
            key = k_ref[n * GROUP : (n + 1) * GROUP, :, lanes].reshape(ROWS, DK)
            query = q_ref[n * GROUP : (n + 1) * GROUP, lanes]
            cum_row, seg_row, rk_row = (table[8 * n + i : 8 * n + i + 1] for i in (0, 2, 5))
            cum_q, seg_q = (columns[:GROUP, 8 * n + i : 8 * n + i + 1] for i in (3, 4))
            raw = dotf(query, key, (((1,), (1,)), ((), ())))
            query32 = query.astype(F32)
            rq = lax.rsqrt(jnp.sum(query32 * query32, axis=1, keepdims=True) + EPS)
            scores = jnp.where(seen & (seg_q == seg_row), raw, 0.0) * (rq * jnp.exp(cum_q)) * (
                rk_row * jnp.exp(-cum_row))
            entry_q = jnp.where(seg_q == prior, jnp.exp(cum_q), 0.0)
            items.append((g, n, query32 * (rq * entry_q), mm_sided(scores, solved_ref[g, n])))
            prior = seg_row[:, ROWS - 1 :]
    for g, n, entering, inner in items:
        rows = slice(n * GROUP, (n + 1) * GROUP)
        lanes = slice(g * DV, (g + 1) * DV)
        reach, local = entering - inner[:, :DK], inner[:, DK:]
        if n:
            joined = mm_sided(reach, prefix_ref[g, n - 1])
            reach, local = joined[:, :DK], local + joined[:, DK:]
        map_ref[rows, lanes] = reach
        out_ref[rows, lanes] = local


KEY_STEP = 4
QUERY_STEP = 2


def key_stage(keys, values, betas, log_decay, segment, step=None):
    tok, heads = keys.shape[0], betas.shape[1]
    blocks = tok // GROUP
    assert blocks == 4
    step = step or KEY_STEP
    body = lambda *refs: key_kernel(step, blocks, *refs)
    return pl.pallas_call(
        body,
        grid=(heads // step,),
        in_specs=[
            pl.BlockSpec((tok, 2, step * DK), lambda h: (0, 0, h)),
            pl.BlockSpec((tok, 2, step * DV), lambda h: (0, 0, h)),
            pl.BlockSpec((2, heads, tok), lambda h: (0, 0, 0)),
            pl.BlockSpec((heads, tok), lambda h: (0, 0)),
            pl.BlockSpec((1, tok), lambda h: (0, 0)),
        ],
        out_specs=[
            pl.BlockSpec((step, DK + 8, DK + DV), lambda h: (h, 0, 0)),
            pl.BlockSpec((step, blocks, ROWS, 2 * (DK + DV)), lambda h: (h, 0, 0, 0)),
            pl.BlockSpec((step, blocks - 1, DK, 2 * (DK + DV)), lambda h: (h, 0, 0, 0)),
            pl.BlockSpec((heads, 8 * blocks, ROWS), lambda h: (0, 0, 0)),
        ],
        out_shape=[
            jax.ShapeDtypeStruct((heads, DK + 8, DK + DV), F32),
            jax.ShapeDtypeStruct((heads, blocks, ROWS, 2 * (DK + DV)), BF16),
            jax.ShapeDtypeStruct((heads, blocks - 1, DK, 2 * (DK + DV)), BF16),
            jax.ShapeDtypeStruct((heads, 8 * blocks, ROWS), F32),
        ],
        compiler_params=pltpu.CompilerParams(dimension_semantics=("arbitrary",)),
        name="key_stage",
    )(keys, values, betas, log_decay, segment.reshape(1, tok))


def query_stage(queries, keys, solved, prefix, table, step=None):
    tok = queries.shape[0]
    heads, blocks = solved.shape[:2]
    step = step or QUERY_STEP
    body = lambda *refs: query_kernel(step, blocks, *refs)
    return pl.pallas_call(
        body,
        grid=(heads // step,),
        in_specs=[
            pl.BlockSpec((tok, step * DK), lambda h: (0, h)),
            pl.BlockSpec((tok, 2, step * DK), lambda h: (0, 0, h)),
            pl.BlockSpec((step, blocks, ROWS, 2 * (DK + DV)), lambda h: (h, 0, 0, 0)),
            pl.BlockSpec((step, blocks - 1, DK, 2 * (DK + DV)), lambda h: (h, 0, 0, 0)),
            pl.BlockSpec((step, 8 * blocks, ROWS), lambda h: (h, 0, 0)),
        ],
        out_specs=[
            pl.BlockSpec((tok, step * DV), lambda h: (0, h)),
            pl.BlockSpec((tok, step * DK), lambda h: (0, h)),
        ],
        out_shape=[
            jax.ShapeDtypeStruct((tok, heads * DV), F32),
            pltpu.VMEM((tok, heads * DK), F32),
        ],
        compiler_params=pltpu.CompilerParams(dimension_semantics=("arbitrary",)),
        name="query_stage",
    )(queries, keys, solved, prefix, table)


def prefix_kernel(in_ref, ex_ref, end_ref, ends_ref):
    count = in_ref.shape[0]
    flags = [jnp.where(in_ref[i, DK : DK + 1, :] == in_ref[i - 1, DK + 1 : DK + 2, :], 1.0, 0.0)
             for i in range(1, count)]
    maps = [in_ref[i, :DK, :DK] * (1.0 if i == 0 else flags[i - 1][:, :DK]) for i in range(count)]
    adds = [in_ref[i, :DK, DK:] for i in range(count)]
    width = 1
    while width < count:
        new_maps, new_adds = list(maps), list(adds)
        for i in range(count):
            if i & width:
                j = (i // width) * width - 1
                joined = mm(maps[i], jnp.concatenate([maps[j], adds[j]], axis=1))
                new_maps[i] = joined[:, :DK]
                new_adds[i] = joined[:, DK:] + adds[i]
        maps, adds = new_maps, new_adds
        width *= 2
    r, c = iota((DK, DK), 0), iota((DK, DK), 1)
    ex_ref[0, :, :DK] = (r == c).astype(F32)
    ex_ref[0, :, DK:] = jnp.zeros((DK, DV), F32)
    for i in range(1, count):
        ex_ref[i, :, :DK] = maps[i - 1] * flags[i - 1][:, :DK]
        ex_ref[i, :, DK:] = adds[i - 1] * flags[i - 1][:, DK:]
    end_ref[:DK, :] = adds[count - 1]
    end_ref[DK:, :] = in_ref[count - 1, DK:, :DV]
    ends_ref[...] = in_ref[0, DK:, :DV]


def incoming_kernel(ends_ref, ex_ref, end_ref, out_ref):
    flag = jnp.where(ends_ref[0:1, :] == end_ref[DK + 1 : DK + 2, :], 1.0, 0.0)
    state = end_ref[:DK, :] * flag
    for i in range(ex_ref.shape[0]):
        out_ref[i] = mm(ex_ref[i, :, :DK], state) + ex_ref[i, :, DK:]


def far_kernel(pick_ref, local_ref, map_ref, state_ref, gain_ref, weight_ref, normed_ref, up_ref, down_ref):
    heads = state_ref.shape[0]

    @pl.when(pl.program_id(0) == 0)
    def _():
        for h in range(heads):
            lanes = slice(h * DV, (h + 1) * DV)
            attended = local_ref[:, lanes] + mm(map_ref[:, lanes], state_ref[h])
            mean = jnp.mean(attended * attended, axis=1, keepdims=True)
            normed_ref[:, lanes] = (attended * lax.rsqrt(mean + EPS) * gain_ref[:, lanes]).astype(BF16)

    half = up_ref.shape[0]
    up_ref[...] = dotf(normed_ref[:half, :], weight_ref[...])
    down_ref[...] = dotf(normed_ref[half:, :], weight_ref[...])


def tile_kernel(pick_ref, normed_ref, weight_ref, top_ref, bottom_ref):
    half = top_ref.shape[0]
    top_ref[...] = dotf(normed_ref[:half, :], weight_ref[...])
    bottom_ref[...] = dotf(normed_ref[half:, :], weight_ref[...])


def whole(*shape):
    return pl.BlockSpec(shape, lambda i, *_: (0,) * len(shape))


def far_tile(place, local, mapped, state, gain, weight, width):
    tok, feats = local.shape
    part = pltpu.VMEM((tok // 2, width), F32)
    steps = 4
    cols = width // steps
    out = pl.BlockSpec((tok // 2, cols), lambda i, at: (0, i))
    return pl.pallas_call(
        far_kernel,
        grid_spec=pltpu.PrefetchScalarGridSpec(
            num_scalar_prefetch=1, grid=(steps,),
            in_specs=[whole(tok, feats), resident(), resident(), whole(1, feats),
                      pl.BlockSpec((feats, cols), lambda i, at: (0, steps * ((at[0] + 2) & 3) + i))],
            out_specs=[whole(tok, feats), out, out]),
        out_shape=[jax.ShapeDtypeStruct((tok, feats), BF16), part, part],
        compiler_params=pltpu.CompilerParams(vmem_limit_bytes=57 << 20),
        name="far_tile",
    )(place, local, held(mapped), held(state), gain.reshape(1, feats), weight)


def join_kernel(nt_ref, gt_ref, lb_ref, gb_ref, top_ref, bottom_ref):
    top_ref[...] = nt_ref[...] + gt_ref[...]
    bottom_ref[...] = lb_ref[...] + gb_ref[...]


def joined(next_top, got_top, last_bottom, got_bottom):
    return pl.pallas_call(
        join_kernel,
        in_specs=[resident()] * 4,
        out_specs=[resident()] * 2,
        out_shape=[pltpu.VMEM(next_top.shape, F32)] * 2,
        compiler_params=pltpu.CompilerParams(vmem_limit_bytes=57 << 20),
        name="join_tiles",
    )(held(next_top), held(got_top), held(last_bottom), held(got_bottom))


def join_kernel(nt_ref, gt_ref, lb_ref, gb_ref, top_ref, bottom_ref):
    top_ref[...] = nt_ref[...] + gt_ref[...]
    bottom_ref[...] = lb_ref[...] + gb_ref[...]


def joined(next_top, got_top, last_bottom, got_bottom):
    return pl.pallas_call(
        join_kernel,
        in_specs=[resident()] * 4,
        out_specs=[resident()] * 2,
        out_shape=[pltpu.VMEM(next_top.shape, F32)] * 2,
        compiler_params=pltpu.CompilerParams(vmem_limit_bytes=57 << 20),
        name="join_tiles",
    )(held(next_top), held(got_top), held(last_bottom), held(got_bottom))


def one_tile(place, normed, weight, width):
    tok, feats = normed.shape
    part = pltpu.VMEM((tok // 2, width), F32)
    cols = width // 2
    out = pl.BlockSpec((tok // 2, cols), lambda i, at: (0, i))
    return pl.pallas_call(
        tile_kernel,
        grid_spec=pltpu.PrefetchScalarGridSpec(
            num_scalar_prefetch=1, grid=(2,),
            in_specs=[whole(tok, feats), pl.BlockSpec((feats, cols), lambda i, at: (0, 2 * at[0] + i))],
            out_specs=[out, out]),
        out_shape=[part, part],
        compiler_params=pltpu.CompilerParams(vmem_limit_bytes=57 << 20),
    )(place, normed, weight)


def sides_kernel(pick_ref, normed_ref, next_w_ref, last_w_ref, nb_ref, lt_ref, nt_ref, lb_ref):
    half = nb_ref.shape[0]
    top, bottom = normed_ref[:half, :], normed_ref[half:, :]
    nb_ref[...] = dotf(bottom, next_w_ref[...])
    lt_ref[...] = dotf(top, last_w_ref[...])
    nt_ref[...] = dotf(top, next_w_ref[...])
    lb_ref[...] = dotf(bottom, last_w_ref[...])


def side_tiles(places, normed, weight, width):
    tok, feats = normed.shape
    steps = 4
    cols = width // steps
    part = jax.ShapeDtypeStruct((tok // 2, width), F32)
    out = pl.BlockSpec((tok // 2, cols), lambda i, at: (0, i))
    return pl.pallas_call(
        sides_kernel,
        grid_spec=pltpu.PrefetchScalarGridSpec(
            num_scalar_prefetch=1, grid=(steps,),
            in_specs=[whole(tok, feats),
                      pl.BlockSpec((feats, cols), lambda i, at: (0, steps * ((at[0] + 1) & 3) + i)),
                      pl.BlockSpec((feats, cols), lambda i, at: (0, steps * ((at[0] + 3) & 3) + i))],
            out_specs=[out] * 4),
        out_shape=[part] * 2 + [pltpu.VMEM((tok // 2, width), F32)] * 2,
        compiler_params=pltpu.CompilerParams(vmem_limit_bytes=57 << 20),
        name="side_tiles",
    )(places, normed, weight, weight)


def finish_kernel(ot_ref, st_ref, gt_ref, ob_ref, sb_ref, gb_ref, out_ref):
    half = ot_ref.shape[0]
    out_ref[:half, :] = (ot_ref[...] + st_ref[...] + gt_ref[...]).astype(BF16)
    out_ref[half:, :] = (ob_ref[...] + sb_ref[...] + gb_ref[...]).astype(BF16)


def summed_output(local, mapped, states, gain, out_weight):
    count = lax.axis_size("head")
    assert count == 4
    mine = lax.axis_index("head")
    width = out_weight.shape[1] // count
    rise = [(i, (i + 1) % count) for i in range(count)]
    fall = [(i, (i - 1) % count) for i in range(count)]
    at = lambda step: ((mine + step) & (count - 1)).astype(jnp.int32).reshape(1)
    up = lambda x: lax.ppermute(x, "head", rise)
    down = lambda x: lax.ppermute(x, "head", fall)
    normed, far_top, far_bottom = far_tile(at(0), local, mapped, states, gain, out_weight, width)
    got_top, got_bottom = up(far_top), down(far_bottom)
    next_bottom, last_top, next_top, last_bottom = side_tiles(
        at(0), normed, out_weight, width)
    side_bottom = up(next_bottom)
    side_top = down(last_top)
    next_top, last_bottom = joined(next_top, got_top, last_bottom, got_bottom)
    got_top, got_bottom = up(next_top), down(last_bottom)
    own_top, own_bottom = one_tile(at(0), normed, out_weight, width)
    return pl.pallas_call(
        finish_kernel,
        in_specs=[resident()] * 6,
        out_shape=jax.ShapeDtypeStruct((2 * own_top.shape[0], width), BF16),
        compiler_params=pltpu.CompilerParams(vmem_limit_bytes=57 << 20),
        name="finish",
    )(*map(held, (own_top, side_top, got_top, own_bottom, side_bottom, got_bottom)))


def shards(queries, keys, values, betas, log_decay, segment, gain, out_weight):
    tok, heads = queries.shape[0], betas.shape[1]
    devices = lax.axis_size("ctx")
    span = DOCUMENT_LIMIT // tok
    assert span == heads and devices % span == 0
    groups = [list(range(i, i + span)) for i in range(0, devices, span)]
    pair, solved, prefix, table = key_stage(keys, values, betas, log_decay, segment)
    local, mapped = query_stage(queries, keys, solved, prefix, table)
    mine = lax.all_to_all(pair, "ctx", 0, 0, axis_index_groups=groups)
    mine, local, mapped = lax.optimization_barrier((mine, local, mapped))
    exclusive, end, ends = pl.pallas_call(
        prefix_kernel,
        in_specs=[resident()],
        out_specs=[resident(), resident(), resident()],
        out_shape=[pltpu.VMEM((span, DK, DK + DV), F32), pltpu.VMEM((DK + 8, DV), F32),
                   pltpu.VMEM((8, DV), F32)],
        compiler_params=pltpu.CompilerParams(vmem_limit_bytes=57 << 20),
        name="prefix_stage",
    )(held(mine))
    end = lax.ppermute(end, "ctx", [(i, i + span) for i in range(devices - span)])
    states = pl.pallas_call(
        incoming_kernel,
        in_specs=[resident(), resident(), resident()],
        out_specs=resident(),
        out_shape=pltpu.VMEM((span, DK, DV), F32),
        compiler_params=pltpu.CompilerParams(vmem_limit_bytes=57 << 20),
        name="incoming_stage",
    )(held(ends), held(exclusive), held(end))
    states = lax.all_to_all(states, "ctx", 0, 0, axis_index_groups=groups)
    return summed_output(local, mapped, states, gain, out_weight)


def solution(mesh):
    return jax.shard_map(
        shards,
        mesh=mesh,
        in_specs=(
            P("ctx", "head"),
            P("ctx", None, "head"),
            P("ctx", None, "head"),
            P(None, "head", "ctx"),
            P("head", "ctx"),
            P("ctx"),
            P("head"),
            P("head", None),
        ),
        out_specs=P("ctx", "head"),
        check_vma=False,
    )
```

```python
import jax
import jax.numpy as jnp
from jax import lax
from jax.experimental import pallas as pl
from jax.experimental.pallas import tpu as pltpu
from jax.sharding import PartitionSpec as P


DK = 128
DV = 128
GROUP = 64
ROWS = 2 * GROUP
DOCUMENT_LIMIT = 2048
EPS = 1e-06
F32 = jnp.float32
BF16 = jnp.bfloat16


def dotf(a, b, dims=(((1,), (0,)), ((), ()))):
    return lax.dot_general(a, b, dims, preferred_element_type=F32)


def halves(x):
    hi = x.astype(BF16)
    lo = (x - hi.astype(F32)).astype(BF16)
    return hi, lo


def side(x):
    return jnp.concatenate(halves(x), axis=1)


def mm(a, b):
    left = side(a)
    outs = []
    for c in range(0, b.shape[1], 128):
        right = side(b[:, c : c + 128])
        r = dotf(left, jnp.concatenate([right, right], axis=0))
        outs.append(r[:, :128] + r[:, 128:])
    return outs[0] if len(outs) == 1 else jnp.concatenate(outs, axis=1)


def mm_tall(a, b):
    m = a.shape[0]
    r = dotf(jnp.concatenate(halves(a), axis=0), side(b))
    return r[:m, :128] + (r[:m, 128:] + r[m:, :128])


def mm_exact_right(a, b16):
    return dotf(side(a), jnp.concatenate([b16, b16], axis=0))


def iota(shape, dim):
    return lax.broadcasted_iota(jnp.int32, shape, dim)


def invert(systems):
    r, c = iota((ROWS, ROWS), 0), iota((ROWS, ROWS), 1)
    eye = (r == c).astype(F32)
    pair = (r >> 1) == (c >> 1)
    xs = [eye - jnp.where(pair, s, 0.0) for s in systems]
    shift = 1
    while (1 << shift) < ROWS:
        band = ((r >> (shift + 1)) == (c >> (shift + 1))) & ((r >> shift) != (c >> shift))
        if shift < 3:
            ys = [mm(jnp.where(band, s, 0.0), x) for s, x in zip(systems, xs)]
            xs = [x - mm(x, y) for x, y in zip(xs, ys)]
        else:
            size = 1 << shift
            low = lambda m: jnp.concatenate(
                [m[i : i + size] for i in range(size, ROWS, 2 * size)], axis=0)

            def spread(m, rest):
                parts = []
                for i in range(ROWS // (2 * size)):
                    parts += [rest(i), m[i * size : (i + 1) * size]]
                return jnp.concatenate(parts, axis=0)

            empty = jnp.zeros((size, ROWS), F32)
            low_band = low(band.astype(F32))
            ys = [mm_tall(low(s) * low_band, x) for s, x in zip(systems, xs)]
            ys = [spread(y, lambda i: empty) for y in ys]
            lows = [low(x) for x in xs]
            lows = [x - mm_tall(x, y) for x, y in zip(lows, ys)]
            xs = [spread(y, lambda i: x[2 * i * size : (2 * i + 1) * size])
                  for x, y in zip(xs, lows)]
        shift += 1
    return xs


def key_kernel(heads_step, blocks, k_ref, v_ref, beta_ref, log_ref, seg_ref,
               pair_ref, solved_ref, prefix_ref, tab_ref):
    step = pl.program_id(0)
    heads = log_ref.shape[0]

    @pl.when(step == 0)
    def _():
        t, s = iota((GROUP, ROWS), 0), iota((GROUP, ROWS), 1)
        even = (s == 2 * t).astype(F32)
        odd = (s == 2 * t + 1).astype(F32)
        upto = (t <= (s >> 1)).astype(F32)
        flat = (t <= s).astype(F32)
        same = (s == t).astype(F32)
        both = even + odd

        def pick(x, sel):
            return lax.dot_general(x, sel, (((1,), (0,)), ((), ())),
                                   precision=lax.Precision.HIGHEST, preferred_element_type=F32)

        def stacked(x):
            return jnp.concatenate([x[:, n * GROUP : (n + 1) * GROUP] for n in range(blocks)], axis=0)

        seg = stacked(jnp.broadcast_to(seg_ref[...].astype(F32), (heads, blocks * GROUP)))
        lg = stacked(log_ref[...])
        kinds = (pick(lg, upto),
                 pick(stacked(beta_ref[0]), even) + pick(stacked(beta_ref[1]), odd),
                 pick(seg, both), pick(lg, flat), pick(seg, same))
        for n in range(blocks):
            for i, kind in enumerate(kinds):
                tab_ref[:, 8 * n + i, :] = kind[n * heads : (n + 1) * heads]
            for z in range(len(kinds), 8):
                tab_ref[:, 8 * n + z, :] = jnp.zeros((heads, ROWS), F32)

    r, c = iota((ROWS, ROWS), 0), iota((ROWS, ROWS), 1)
    diag = r == c
    eye = diag.astype(F32)
    strictly = r > c

    items = []
    for g in range(heads_step):
        lanes = slice(g * DK, (g + 1) * DK)
        table = tab_ref[step * heads_step + g]
        columns = columns_of(table, blocks)
        prior = table[2:3, 0:1]
        for n in range(blocks):
            key = k_ref[n * GROUP : (n + 1) * GROUP, :, lanes].reshape(ROWS, DK)
            value = v_ref[n * GROUP : (n + 1) * GROUP, :, lanes].reshape(ROWS, DV)
            cum_row, beta_row, seg_row = (table[8 * n + i : 8 * n + i + 1] for i in range(3))
            cum_col, beta_col, seg_col = (columns[:, 8 * n + i : 8 * n + i + 1] for i in range(3))
            cum_last, seg_last = cum_row[:, ROWS - 1 :], seg_row[:, ROWS - 1 :]
            raw = dotf(key, key, (((1,), (1,)), ((), ())))
            own = jnp.where(diag, raw, 0.0)
            rk_row = lax.rsqrt(jnp.sum(own, axis=0, keepdims=True) + EPS)
            rk_col = lax.rsqrt(jnp.sum(own, axis=1, keepdims=True) + EPS)
            tab_ref[step * heads_step + g, 8 * n + 5 : 8 * n + 6, :] = rk_row
            system = jnp.where(strictly & (seg_col == seg_row), raw, 0.0) * (
                beta_col * rk_col * jnp.exp(cum_col)) * (rk_row * jnp.exp(-cum_row))
            entry_row = jnp.where(seg_row == prior, jnp.exp(cum_row), 0.0)
            tail_col = jnp.where(seg_col == seg_last, jnp.exp(cum_last - cum_col), 0.0) * rk_col
            tail_entry = jnp.where(seg_last == prior, jnp.exp(cum_last), 0.0)
            items.append(dict(
                g=g, n=n, key=key, value=value, system=system, wv=beta_row,
                wk=beta_row * rk_row * entry_row, tail=tail_col, tail_entry=tail_entry))
            prior = seg_last

    for item, x in zip(items, invert([item["system"] for item in items])):
        item["pseudo"] = mm_exact_right(x * item["wv"], item["value"])
        item["key_mix"] = mm_exact_right(x * item["wk"], item["key"])
    for item in items:
        g, n = item["g"], item["n"]
        both = jnp.concatenate([item["key_mix"], item["pseudo"]], axis=1)
        solved_ref[g, n] = side(both)
        r2 = dotf(item["key"], side(both * item["tail"]), (((0,), (0,)), ((), ())))
        r2 = r2[:, : 2 * DK] + r2[:, 2 * DK :]
        item["pair"] = (item["tail_entry"] * eye - r2[:, :DK], r2[:, DK:])

    def after(later, earlier):
        joined = mm(later[0], jnp.concatenate(earlier, axis=1))
        return joined[:, :DK], joined[:, DK:] + later[1]

    totals = [[items[g * blocks + n]["pair"] for n in range(blocks)] for g in range(heads_step)]
    first, halfway, third = [t[0] for t in totals], [], []
    halfway = [after(t[1], t[0]) for t in totals]
    upper = [after(t[3], t[2]) for t in totals]
    third = [after(t[2], h) for t, h in zip(totals, halfway)]
    final = [after(u, h) for u, h in zip(upper, halfway)]
    begin = seg_ref[:, 0:1].astype(F32)
    last = seg_ref[:, blocks * GROUP - 1 :].astype(F32)
    ends = jnp.where(iota((8, 2 * DK), 0) == 0, begin, last)
    for g in range(heads_step):
        for n, pair in enumerate((first[g], halfway[g], third[g])):
            prefix_ref[g, n] = side(jnp.concatenate(pair, axis=1))
        pair_ref[g, :DK, :DK] = final[g][0]
        pair_ref[g, :DK, DK:] = final[g][1]
        pair_ref[g, DK:, :] = ends


def resident():
    return pl.BlockSpec(memory_space=pltpu.VMEM)


def held(x):
    return pltpu.with_memory_space_constraint(x, pltpu.VMEM)


def columns_of(table, blocks):
    return jnp.concatenate([table, jnp.zeros((ROWS - 8 * blocks, ROWS), F32)], axis=0).T


def mm_sided(a, right):
    width = right.shape[1] // 2
    r = dotf(side(a), jnp.concatenate([right, right], axis=0))
    return r[:, :width] + r[:, width:]


def query_kernel(heads_step, blocks, q_ref, k_ref, solved_ref, prefix_ref, tab_ref, out_ref, map_ref):
    qr, qc = iota((GROUP, ROWS), 0), iota((GROUP, ROWS), 1)
    seen = qc <= 2 * qr + 1
    items = []
    for g in range(heads_step):
        lanes = slice(g * DK, (g + 1) * DK)
        table = tab_ref[g]
        columns = columns_of(table, blocks)
        prior = table[2:3, 0:1]
        for n in range(blocks):
            key = k_ref[n * GROUP : (n + 1) * GROUP, :, lanes].reshape(ROWS, DK)
            query = q_ref[n * GROUP : (n + 1) * GROUP, lanes]
            cum_row, seg_row, rk_row = (table[8 * n + i : 8 * n + i + 1] for i in (0, 2, 5))
            cum_q, seg_q = (columns[:GROUP, 8 * n + i : 8 * n + i + 1] for i in (3, 4))
            raw = dotf(query, key, (((1,), (1,)), ((), ())))
            query32 = query.astype(F32)
            rq = lax.rsqrt(jnp.sum(query32 * query32, axis=1, keepdims=True) + EPS)
            scores = jnp.where(seen & (seg_q == seg_row), raw, 0.0) * (rq * jnp.exp(cum_q)) * (
                rk_row * jnp.exp(-cum_row))
            entry_q = jnp.where(seg_q == prior, jnp.exp(cum_q), 0.0)
            items.append((g, n, query32 * (rq * entry_q), mm_sided(scores, solved_ref[g, n])))
            prior = seg_row[:, ROWS - 1 :]
    for g, n, entering, inner in items:
        rows = slice(n * GROUP, (n + 1) * GROUP)
        lanes = slice(g * DV, (g + 1) * DV)
        reach, local = entering - inner[:, :DK], inner[:, DK:]
        if n:
            joined = mm_sided(reach, prefix_ref[g, n - 1])
            reach, local = joined[:, :DK], local + joined[:, DK:]
        map_ref[rows, lanes] = reach
        out_ref[rows, lanes] = local


KEY_STEP = 4
QUERY_STEP = 2


def key_stage(keys, values, betas, log_decay, segment, step=None):
    tok, heads = keys.shape[0], betas.shape[1]
    blocks = tok // GROUP
    assert blocks == 4
    step = step or KEY_STEP
    body = lambda *refs: key_kernel(step, blocks, *refs)
    return pl.pallas_call(
        body,
        grid=(heads // step,),
        in_specs=[
            pl.BlockSpec((tok, 2, step * DK), lambda h: (0, 0, h)),
            pl.BlockSpec((tok, 2, step * DV), lambda h: (0, 0, h)),
            pl.BlockSpec((2, heads, tok), lambda h: (0, 0, 0)),
            pl.BlockSpec((heads, tok), lambda h: (0, 0)),
            pl.BlockSpec((1, tok), lambda h: (0, 0)),
        ],
        out_specs=[
            pl.BlockSpec((step, DK + 8, DK + DV), lambda h: (h, 0, 0)),
            pl.BlockSpec((step, blocks, ROWS, 2 * (DK + DV)), lambda h: (h, 0, 0, 0)),
            pl.BlockSpec((step, blocks - 1, DK, 2 * (DK + DV)), lambda h: (h, 0, 0, 0)),
            pl.BlockSpec((heads, 8 * blocks, ROWS), lambda h: (0, 0, 0)),
        ],
        out_shape=[
            jax.ShapeDtypeStruct((heads, DK + 8, DK + DV), F32),
            jax.ShapeDtypeStruct((heads, blocks, ROWS, 2 * (DK + DV)), BF16),
            jax.ShapeDtypeStruct((heads, blocks - 1, DK, 2 * (DK + DV)), BF16),
            jax.ShapeDtypeStruct((heads, 8 * blocks, ROWS), F32),
        ],
        compiler_params=pltpu.CompilerParams(dimension_semantics=("arbitrary",)),
        name="key_stage",
    )(keys, values, betas, log_decay, segment.reshape(1, tok))


def query_stage(queries, keys, solved, prefix, table, step=None):
    tok = queries.shape[0]
    heads, blocks = solved.shape[:2]
    step = step or QUERY_STEP
    body = lambda *refs: query_kernel(step, blocks, *refs)
    return pl.pallas_call(
        body,
        grid=(heads // step,),
        in_specs=[
            pl.BlockSpec((tok, step * DK), lambda h: (0, h)),
            pl.BlockSpec((tok, 2, step * DK), lambda h: (0, 0, h)),
            pl.BlockSpec((step, blocks, ROWS, 2 * (DK + DV)), lambda h: (h, 0, 0, 0)),
            pl.BlockSpec((step, blocks - 1, DK, 2 * (DK + DV)), lambda h: (h, 0, 0, 0)),
            pl.BlockSpec((step, 8 * blocks, ROWS), lambda h: (h, 0, 0)),
        ],
        out_specs=[
            pl.BlockSpec((tok, step * DV), lambda h: (0, h)),
            pl.BlockSpec((tok, step * DK), lambda h: (0, h)),
        ],
        out_shape=[
            jax.ShapeDtypeStruct((tok, heads * DV), F32),
            pltpu.VMEM((tok, heads * DK), F32),
        ],
        compiler_params=pltpu.CompilerParams(dimension_semantics=("arbitrary",)),
        name="query_stage",
    )(queries, keys, solved, prefix, table)


def prefix_kernel(in_ref, ex_ref, end_ref, ends_ref):
    count = in_ref.shape[0]
    flags = [jnp.where(in_ref[i, DK : DK + 1, :] == in_ref[i - 1, DK + 1 : DK + 2, :], 1.0, 0.0)
             for i in range(1, count)]
    maps = [in_ref[i, :DK, :DK] * (1.0 if i == 0 else flags[i - 1][:, :DK]) for i in range(count)]
    adds = [in_ref[i, :DK, DK:] for i in range(count)]
    width = 1
    while width < count:
        new_maps, new_adds = list(maps), list(adds)
        for i in range(count):
            if i & width:
                j = (i // width) * width - 1
                joined = mm(maps[i], jnp.concatenate([maps[j], adds[j]], axis=1))
                new_maps[i] = joined[:, :DK]
                new_adds[i] = joined[:, DK:] + adds[i]
        maps, adds = new_maps, new_adds
        width *= 2
    r, c = iota((DK, DK), 0), iota((DK, DK), 1)
    ex_ref[0, :, :DK] = (r == c).astype(F32)
    ex_ref[0, :, DK:] = jnp.zeros((DK, DV), F32)
    for i in range(1, count):
        ex_ref[i, :, :DK] = maps[i - 1] * flags[i - 1][:, :DK]
        ex_ref[i, :, DK:] = adds[i - 1] * flags[i - 1][:, DK:]
    end_ref[:DK, :] = adds[count - 1]
    end_ref[DK:, :] = in_ref[count - 1, DK:, :DV]
    ends_ref[...] = in_ref[0, DK:, :DV]


def incoming_kernel(spot_ref, ends_ref, ex_ref, end_ref, *out_refs):
    flag = jnp.where(ends_ref[0:1, :] == end_ref[DK + 1 : DK + 2, :], 1.0, 0.0)
    state = end_ref[:DK, :] * flag
    for step, out_ref in enumerate(out_refs):
        i = spot_ref[0] ^ step
        out_ref[...] = mm(ex_ref[i, :, :DK], state) + ex_ref[i, :, DK:]


def far_kernel(heads, place_ref, spot_ref, local_ref, map_ref, gain_ref, weight_ref, *refs):
    state_refs = refs[:heads]
    normed_ref, up_ref, down_ref, columns_ref, own_ref, copied, read = refs[heads:]
    width = up_ref.shape[1]
    start = pl.multiple_of(((place_ref[0] + 2) & 3) * width, width)
    bring = pltpu.make_async_copy(local_ref, own_ref, read)
    bring.start()
    load = pltpu.make_async_copy(weight_ref.at[:, pl.ds(start, width)], columns_ref, copied)
    load.start()
    spots = [pl.ds(pl.multiple_of((spot_ref[0] ^ step) * DV, DV), DV) for step in range(heads)]
    read_out = [mm(map_ref[:, lanes], ref[...]) for lanes, ref in zip(spots, state_refs)]
    bring.wait()
    for lanes, part in zip(spots, read_out):
        attended = own_ref[:, lanes] + part
        mean = jnp.mean(attended * attended, axis=1, keepdims=True)
        normed_ref[:, lanes] = (attended * lax.rsqrt(mean + EPS) * gain_ref[:, lanes]).astype(BF16)
    load.wait()
    half = up_ref.shape[0]
    up_ref[...] = dotf(normed_ref[:half, :], columns_ref[...])
    down_ref[...] = dotf(normed_ref[half:, :], columns_ref[...])


def tile_kernel(pick_ref, normed_ref, weight_ref, top_ref, bottom_ref):
    half = top_ref.shape[0]
    top_ref[...] = dotf(normed_ref[:half, :], weight_ref[...])
    bottom_ref[...] = dotf(normed_ref[half:, :], weight_ref[...])


def whole(*shape):
    return pl.BlockSpec(shape, lambda i, *_: (0,) * len(shape))


def far_tile(place, spot, local, mapped, states, gain, weight, width):
    tok, feats = local.shape
    part = pltpu.VMEM((tok // 2, width), F32)
    anywhere = pl.BlockSpec(memory_space=pl.ANY)
    scalar = pl.BlockSpec(memory_space=pltpu.SMEM)
    body = lambda *refs: far_kernel(len(states), *refs)
    return pl.pallas_call(
        body,
        in_specs=[scalar, scalar, anywhere, resident(), resident(), anywhere] + [resident()] * len(states),
        out_specs=[resident()] * 3,
        out_shape=[jax.ShapeDtypeStruct((tok, feats), BF16), part, part],
        scratch_shapes=[pltpu.VMEM((feats, width), BF16), pltpu.VMEM((tok, feats), F32),
                        pltpu.SemaphoreType.DMA(()), pltpu.SemaphoreType.DMA(())],
        compiler_params=pltpu.CompilerParams(vmem_limit_bytes=57 << 20),
        name="far_tile",
    )(place, spot, local, held(mapped), gain.reshape(1, feats), weight, *map(held, states))


def join_kernel(nt_ref, gt_ref, lb_ref, gb_ref, top_ref, bottom_ref):
    top_ref[...] = nt_ref[...] + gt_ref[...]
    bottom_ref[...] = lb_ref[...] + gb_ref[...]


def joined(next_top, got_top, last_bottom, got_bottom):
    return pl.pallas_call(
        join_kernel,
        in_specs=[resident()] * 4,
        out_specs=[resident()] * 2,
        out_shape=[pltpu.VMEM(next_top.shape, F32)] * 2,
        compiler_params=pltpu.CompilerParams(vmem_limit_bytes=57 << 20),
        name="join_tiles",
    )(held(next_top), held(got_top), held(last_bottom), held(got_bottom))


def join_kernel(nt_ref, gt_ref, lb_ref, gb_ref, top_ref, bottom_ref):
    top_ref[...] = nt_ref[...] + gt_ref[...]
    bottom_ref[...] = lb_ref[...] + gb_ref[...]


def joined(next_top, got_top, last_bottom, got_bottom):
    return pl.pallas_call(
        join_kernel,
        in_specs=[resident()] * 4,
        out_specs=[resident()] * 2,
        out_shape=[pltpu.VMEM(next_top.shape, F32)] * 2,
        compiler_params=pltpu.CompilerParams(vmem_limit_bytes=57 << 20),
        name="join_tiles",
    )(held(next_top), held(got_top), held(last_bottom), held(got_bottom))


def one_tile(place, normed, weight, width):
    tok, feats = normed.shape
    part = pltpu.VMEM((tok // 2, width), F32)
    cols = width // 2
    out = pl.BlockSpec((tok // 2, cols), lambda i, at: (0, i))
    return pl.pallas_call(
        tile_kernel,
        grid_spec=pltpu.PrefetchScalarGridSpec(
            num_scalar_prefetch=1, grid=(2,),
            in_specs=[whole(tok, feats), pl.BlockSpec((feats, cols), lambda i, at: (0, 2 * at[0] + i))],
            out_specs=[out, out]),
        out_shape=[part, part],
        compiler_params=pltpu.CompilerParams(vmem_limit_bytes=57 << 20),
    )(place, normed, weight)


def sides_kernel(pick_ref, normed_ref, next_w_ref, last_w_ref, nb_ref, lt_ref, nt_ref, lb_ref):
    half = nb_ref.shape[0]
    top, bottom = normed_ref[:half, :], normed_ref[half:, :]
    nb_ref[...] = dotf(bottom, next_w_ref[...])
    lt_ref[...] = dotf(top, last_w_ref[...])
    nt_ref[...] = dotf(top, next_w_ref[...])
    lb_ref[...] = dotf(bottom, last_w_ref[...])


def side_tiles(places, normed, weight, width):
    tok, feats = normed.shape
    steps = 4
    cols = width // steps
    part = jax.ShapeDtypeStruct((tok // 2, width), F32)
    out = pl.BlockSpec((tok // 2, cols), lambda i, at: (0, i))
    return pl.pallas_call(
        sides_kernel,
        grid_spec=pltpu.PrefetchScalarGridSpec(
            num_scalar_prefetch=1, grid=(steps,),
            in_specs=[whole(tok, feats),
                      pl.BlockSpec((feats, cols), lambda i, at: (0, steps * ((at[0] + 1) & 3) + i)),
                      pl.BlockSpec((feats, cols), lambda i, at: (0, steps * ((at[0] + 3) & 3) + i))],
            out_specs=[out] * 4),
        out_shape=[part] * 2 + [pltpu.VMEM((tok // 2, width), F32)] * 2,
        compiler_params=pltpu.CompilerParams(vmem_limit_bytes=57 << 20),
        name="side_tiles",
    )(places, normed, weight, weight)


def finish_kernel(ot_ref, st_ref, gt_ref, ob_ref, sb_ref, gb_ref, out_ref):
    half = ot_ref.shape[0]
    out_ref[:half, :] = (ot_ref[...] + st_ref[...] + gt_ref[...]).astype(BF16)
    out_ref[half:, :] = (ob_ref[...] + sb_ref[...] + gb_ref[...]).astype(BF16)


def summed_output(spot, local, mapped, states, gain, out_weight):
    count = lax.axis_size("head")
    assert count == 4
    mine = lax.axis_index("head")
    width = out_weight.shape[1] // count
    rise = [(i, (i + 1) % count) for i in range(count)]
    fall = [(i, (i - 1) % count) for i in range(count)]
    at = lambda step: ((mine + step) & (count - 1)).astype(jnp.int32).reshape(1)
    up = lambda x: lax.ppermute(x, "head", rise)
    down = lambda x: lax.ppermute(x, "head", fall)
    normed, far_top, far_bottom = far_tile(at(0), spot, local, mapped, states, gain, out_weight, width)
    got_top, got_bottom = up(far_top), down(far_bottom)
    next_bottom, last_top, next_top, last_bottom = side_tiles(
        at(0), normed, out_weight, width)
    side_bottom = up(next_bottom)
    side_top = down(last_top)
    next_top, last_bottom = joined(next_top, got_top, last_bottom, got_bottom)
    got_top, got_bottom = up(next_top), down(last_bottom)
    own_top, own_bottom = one_tile(at(0), normed, out_weight, width)
    return pl.pallas_call(
        finish_kernel,
        in_specs=[resident()] * 6,
        out_shape=jax.ShapeDtypeStruct((2 * own_top.shape[0], width), BF16),
        compiler_params=pltpu.CompilerParams(vmem_limit_bytes=57 << 20),
        name="finish",
    )(*map(held, (own_top, side_top, got_top, own_bottom, side_bottom, got_bottom)))


def shards(queries, keys, values, betas, log_decay, segment, gain, out_weight):
    tok, heads = queries.shape[0], betas.shape[1]
    devices = lax.axis_size("ctx")
    span = DOCUMENT_LIMIT // tok
    assert span == heads and devices % span == 0
    groups = [list(range(i, i + span)) for i in range(0, devices, span)]
    pair, solved, prefix, table = key_stage(keys, values, betas, log_decay, segment)
    local, mapped = query_stage(queries, keys, solved, prefix, table)
    mine = lax.all_to_all(pair, "ctx", 0, 0, axis_index_groups=groups)
    mine, local, mapped = lax.optimization_barrier((mine, local, mapped))
    exclusive, end, ends = pl.pallas_call(
        prefix_kernel,
        in_specs=[resident()],
        out_specs=[resident(), resident(), resident()],
        out_shape=[pltpu.VMEM((span, DK, DK + DV), F32), pltpu.VMEM((DK + 8, DV), F32),
                   pltpu.VMEM((8, DV), F32)],
        compiler_params=pltpu.CompilerParams(vmem_limit_bytes=57 << 20),
        name="prefix_stage",
    )(held(mine))
    end = lax.ppermute(end, "ctx", [(i, i + span) for i in range(devices - span)])
    assert span & (span - 1) == 0
    spot = (lax.axis_index("ctx") & (span - 1)).astype(jnp.int32).reshape(1)
    states = pl.pallas_call(
        incoming_kernel,
        in_specs=[pl.BlockSpec(memory_space=pltpu.SMEM)] + [resident()] * 3,
        out_specs=[resident()] * span,
        out_shape=[pltpu.VMEM((DK, DV), F32)] * span,
        compiler_params=pltpu.CompilerParams(vmem_limit_bytes=57 << 20),
        name="incoming_stage",
    )(spot, held(ends), held(exclusive), held(end))
    moved = {step: lax.ppermute(states[step], "ctx", [(i, i ^ step) for i in range(devices)])
             for step in (4, 5, 2, 6, 3, 7, 1)}
    states = [states[0]] + [moved[step] for step in range(1, span)]
    return summed_output(spot, local, mapped, states, gain, out_weight)


def solution(mesh):
    return jax.shard_map(
        shards,
        mesh=mesh,
        in_specs=(
            P("ctx", "head"),
            P("ctx", None, "head"),
            P("ctx", None, "head"),
            P(None, "head", "ctx"),
            P("head", "ctx"),
            P("ctx"),
            P("head"),
            P("head", None),
        ),
        out_specs=P("ctx", "head"),
        check_vma=False,
    )
```

```python
import jax
import jax.numpy as jnp
from jax import lax
from jax.experimental import pallas as pl
from jax.experimental.pallas import tpu as pltpu
from jax.sharding import PartitionSpec as P


DK = 128
DV = 128
GROUP = 64
ROWS = 2 * GROUP
DOCUMENT_LIMIT = 2048
EPS = 1e-06
F32 = jnp.float32
BF16 = jnp.bfloat16


def dotf(a, b, dims=(((1,), (0,)), ((), ()))):
    return lax.dot_general(a, b, dims, preferred_element_type=F32)


def halves(x):
    hi = x.astype(BF16)
    lo = (x - hi.astype(F32)).astype(BF16)
    return hi, lo


def side(x):
    return jnp.concatenate(halves(x), axis=1)


def mm(a, b):
    left = side(a)
    outs = []
    for c in range(0, b.shape[1], 128):
        right = side(b[:, c : c + 128])
        r = dotf(left, jnp.concatenate([right, right], axis=0))
        outs.append(r[:, :128] + r[:, 128:])
    return outs[0] if len(outs) == 1 else jnp.concatenate(outs, axis=1)


def mm_tall(a, b):
    m = a.shape[0]
    r = dotf(jnp.concatenate(halves(a), axis=0), side(b))
    return r[:m, :128] + (r[:m, 128:] + r[m:, :128])


def mm_exact_right(a, b16):
    return dotf(side(a), jnp.concatenate([b16, b16], axis=0))


def iota(shape, dim):
    return lax.broadcasted_iota(jnp.int32, shape, dim)


def invert(systems):
    r, c = iota((ROWS, ROWS), 0), iota((ROWS, ROWS), 1)
    eye = (r == c).astype(F32)
    pair = (r >> 1) == (c >> 1)
    xs = [eye - jnp.where(pair, s, 0.0) for s in systems]
    shift = 1
    while (1 << shift) < ROWS:
        band = ((r >> (shift + 1)) == (c >> (shift + 1))) & ((r >> shift) != (c >> shift))
        if shift < 3:
            ys = [mm(jnp.where(band, s, 0.0), x) for s, x in zip(systems, xs)]
            xs = [x - mm(x, y) for x, y in zip(xs, ys)]
        else:
            size = 1 << shift
            low = lambda m: jnp.concatenate(
                [m[i : i + size] for i in range(size, ROWS, 2 * size)], axis=0)

            def spread(m, rest):
                parts = []
                for i in range(ROWS // (2 * size)):
                    parts += [rest(i), m[i * size : (i + 1) * size]]
                return jnp.concatenate(parts, axis=0)

            empty = jnp.zeros((size, ROWS), F32)
            low_band = low(band.astype(F32))
            ys = [mm_tall(low(s) * low_band, x) for s, x in zip(systems, xs)]
            ys = [spread(y, lambda i: empty) for y in ys]
            lows = [low(x) for x in xs]
            lows = [x - mm_tall(x, y) for x, y in zip(lows, ys)]
            xs = [spread(y, lambda i: x[2 * i * size : (2 * i + 1) * size])
                  for x, y in zip(xs, lows)]
        shift += 1
    return xs


def key_kernel(heads_step, blocks, k_ref, v_ref, beta_ref, log_ref, seg_ref,
               pair_ref, solved_ref, prefix_ref, tab_ref):
    step = pl.program_id(0)
    heads = log_ref.shape[0]

    @pl.when(step == 0)
    def _():
        t, s = iota((GROUP, ROWS), 0), iota((GROUP, ROWS), 1)
        even = (s == 2 * t).astype(F32)
        odd = (s == 2 * t + 1).astype(F32)
        upto = (t <= (s >> 1)).astype(F32)
        flat = (t <= s).astype(F32)
        same = (s == t).astype(F32)
        both = even + odd

        def pick(x, sel):
            return lax.dot_general(x, sel, (((1,), (0,)), ((), ())),
                                   precision=lax.Precision.HIGHEST, preferred_element_type=F32)

        def stacked(x):
            return jnp.concatenate([x[:, n * GROUP : (n + 1) * GROUP] for n in range(blocks)], axis=0)

        seg = stacked(jnp.broadcast_to(seg_ref[...].astype(F32), (heads, blocks * GROUP)))
        lg = stacked(log_ref[...])
        kinds = (pick(lg, upto),
                 pick(stacked(beta_ref[0]), even) + pick(stacked(beta_ref[1]), odd),
                 pick(seg, both), pick(lg, flat), pick(seg, same))
        for n in range(blocks):
            for i, kind in enumerate(kinds):
                tab_ref[:, 8 * n + i, :] = kind[n * heads : (n + 1) * heads]
            for z in range(len(kinds), 8):
                tab_ref[:, 8 * n + z, :] = jnp.zeros((heads, ROWS), F32)

    r, c = iota((ROWS, ROWS), 0), iota((ROWS, ROWS), 1)
    diag = r == c
    eye = diag.astype(F32)
    strictly = r > c

    items = []
    for g in range(heads_step):
        lanes = slice(g * DK, (g + 1) * DK)
        table = tab_ref[step * heads_step + g]
        columns = columns_of(table, blocks)
        prior = table[2:3, 0:1]
        for n in range(blocks):
            key = k_ref[n * GROUP : (n + 1) * GROUP, :, lanes].reshape(ROWS, DK)
            value = v_ref[n * GROUP : (n + 1) * GROUP, :, lanes].reshape(ROWS, DV)
            cum_row, beta_row, seg_row = (table[8 * n + i : 8 * n + i + 1] for i in range(3))
            cum_col, beta_col, seg_col = (columns[:, 8 * n + i : 8 * n + i + 1] for i in range(3))
            cum_last, seg_last = cum_row[:, ROWS - 1 :], seg_row[:, ROWS - 1 :]
            raw = dotf(key, key, (((1,), (1,)), ((), ())))
            own = jnp.where(diag, raw, 0.0)
            rk_row = lax.rsqrt(jnp.sum(own, axis=0, keepdims=True) + EPS)
            rk_col = lax.rsqrt(jnp.sum(own, axis=1, keepdims=True) + EPS)
            tab_ref[step * heads_step + g, 8 * n + 5 : 8 * n + 6, :] = rk_row
            system = jnp.where(strictly & (seg_col == seg_row), raw, 0.0) * (
                beta_col * rk_col * jnp.exp(cum_col)) * (rk_row * jnp.exp(-cum_row))
            entry_row = jnp.where(seg_row == prior, jnp.exp(cum_row), 0.0)
            tail_col = jnp.where(seg_col == seg_last, jnp.exp(cum_last - cum_col), 0.0) * rk_col
            tail_entry = jnp.where(seg_last == prior, jnp.exp(cum_last), 0.0)
            items.append(dict(
                g=g, n=n, key=key, value=value, system=system, wv=beta_row,
                wk=beta_row * rk_row * entry_row, tail=tail_col, tail_entry=tail_entry))
            prior = seg_last

    for item, x in zip(items, invert([item["system"] for item in items])):
        item["pseudo"] = mm_exact_right(x * item["wv"], item["value"])
        item["key_mix"] = mm_exact_right(x * item["wk"], item["key"])
    for item in items:
        g, n = item["g"], item["n"]
        both = jnp.concatenate([item["key_mix"], item["pseudo"]], axis=1)
        solved_ref[g, n] = side(both)
        r2 = dotf(item["key"], side(both * item["tail"]), (((0,), (0,)), ((), ())))
        r2 = r2[:, : 2 * DK] + r2[:, 2 * DK :]
        item["pair"] = (item["tail_entry"] * eye - r2[:, :DK], r2[:, DK:])

    def after(later, earlier):
        joined = mm(later[0], jnp.concatenate(earlier, axis=1))
        return joined[:, :DK], joined[:, DK:] + later[1]

    totals = [[items[g * blocks + n]["pair"] for n in range(blocks)] for g in range(heads_step)]
    first, halfway, third = [t[0] for t in totals], [], []
    halfway = [after(t[1], t[0]) for t in totals]
    upper = [after(t[3], t[2]) for t in totals]
    third = [after(t[2], h) for t, h in zip(totals, halfway)]
    final = [after(u, h) for u, h in zip(upper, halfway)]
    begin = seg_ref[:, 0:1].astype(F32)
    last = seg_ref[:, blocks * GROUP - 1 :].astype(F32)
    ends = jnp.where(iota((8, 2 * DK), 0) == 0, begin, last)
    for g in range(heads_step):
        for n, pair in enumerate((first[g], halfway[g], third[g])):
            prefix_ref[g, n] = side(jnp.concatenate(pair, axis=1))
        pair_ref[g, :DK, :DK] = final[g][0]
        pair_ref[g, :DK, DK:] = final[g][1]
        pair_ref[g, DK:, :] = ends


def resident():
    return pl.BlockSpec(memory_space=pltpu.VMEM)


def held(x):
    return pltpu.with_memory_space_constraint(x, pltpu.VMEM)


def columns_of(table, blocks):
    return jnp.concatenate([table, jnp.zeros((ROWS - 8 * blocks, ROWS), F32)], axis=0).T


def mm_sided(a, right):
    width = right.shape[1] // 2
    r = dotf(side(a), jnp.concatenate([right, right], axis=0))
    return r[:, :width] + r[:, width:]


def query_kernel(heads_step, blocks, q_ref, k_ref, solved_ref, prefix_ref, tab_ref, out_ref, map_ref):
    qr, qc = iota((GROUP, ROWS), 0), iota((GROUP, ROWS), 1)
    seen = qc <= 2 * qr + 1
    items = []
    for g in range(heads_step):
        lanes = slice(g * DK, (g + 1) * DK)
        table = tab_ref[g]
        columns = columns_of(table, blocks)
        prior = table[2:3, 0:1]
        for n in range(blocks):
            key = k_ref[n * GROUP : (n + 1) * GROUP, :, lanes].reshape(ROWS, DK)
            query = q_ref[n * GROUP : (n + 1) * GROUP, lanes]
            cum_row, seg_row, rk_row = (table[8 * n + i : 8 * n + i + 1] for i in (0, 2, 5))
            cum_q, seg_q = (columns[:GROUP, 8 * n + i : 8 * n + i + 1] for i in (3, 4))
            raw = dotf(query, key, (((1,), (1,)), ((), ())))
            query32 = query.astype(F32)
            rq = lax.rsqrt(jnp.sum(query32 * query32, axis=1, keepdims=True) + EPS)
            scores = jnp.where(seen & (seg_q == seg_row), raw, 0.0) * (rq * jnp.exp(cum_q)) * (
                rk_row * jnp.exp(-cum_row))
            entry_q = jnp.where(seg_q == prior, jnp.exp(cum_q), 0.0)
            items.append((g, n, query32 * (rq * entry_q), mm_sided(scores, solved_ref[g, n])))
            prior = seg_row[:, ROWS - 1 :]
    for g, n, entering, inner in items:
        rows = slice(n * GROUP, (n + 1) * GROUP)
        lanes = slice(g * DV, (g + 1) * DV)
        reach, local = entering - inner[:, :DK], inner[:, DK:]
        if n:
            joined = mm_sided(reach, prefix_ref[g, n - 1])
            reach, local = joined[:, :DK], local + joined[:, DK:]
        map_ref[rows, lanes] = reach
        out_ref[rows, lanes] = local


KEY_STEP = 4
QUERY_STEP = 2


def key_stage(keys, values, betas, log_decay, segment, step=None):
    tok, heads = keys.shape[0], betas.shape[1]
    blocks = tok // GROUP
    assert blocks == 4
    step = step or KEY_STEP
    body = lambda *refs: key_kernel(step, blocks, *refs)
    return pl.pallas_call(
        body,
        grid=(heads // step,),
        in_specs=[
            pl.BlockSpec((tok, 2, step * DK), lambda h: (0, 0, h)),
            pl.BlockSpec((tok, 2, step * DV), lambda h: (0, 0, h)),
            pl.BlockSpec((2, heads, tok), lambda h: (0, 0, 0)),
            pl.BlockSpec((heads, tok), lambda h: (0, 0)),
            pl.BlockSpec((1, tok), lambda h: (0, 0)),
        ],
        out_specs=[
            pl.BlockSpec((step, DK + 8, DK + DV), lambda h: (h, 0, 0)),
            pl.BlockSpec((step, blocks, ROWS, 2 * (DK + DV)), lambda h: (h, 0, 0, 0)),
            pl.BlockSpec((step, blocks - 1, DK, 2 * (DK + DV)), lambda h: (h, 0, 0, 0)),
            pl.BlockSpec((heads, 8 * blocks, ROWS), lambda h: (0, 0, 0)),
        ],
        out_shape=[
            jax.ShapeDtypeStruct((heads, DK + 8, DK + DV), F32),
            jax.ShapeDtypeStruct((heads, blocks, ROWS, 2 * (DK + DV)), BF16),
            jax.ShapeDtypeStruct((heads, blocks - 1, DK, 2 * (DK + DV)), BF16),
            jax.ShapeDtypeStruct((heads, 8 * blocks, ROWS), F32),
        ],
        compiler_params=pltpu.CompilerParams(dimension_semantics=("arbitrary",)),
        name="key_stage",
    )(keys, values, betas, log_decay, segment.reshape(1, tok))


def query_stage(queries, keys, solved, prefix, table, step=None):
    tok = queries.shape[0]
    heads, blocks = solved.shape[:2]
    step = step or QUERY_STEP
    body = lambda *refs: query_kernel(step, blocks, *refs)
    return pl.pallas_call(
        body,
        grid=(heads // step,),
        in_specs=[
            pl.BlockSpec((tok, step * DK), lambda h: (0, h)),
            pl.BlockSpec((tok, 2, step * DK), lambda h: (0, 0, h)),
            pl.BlockSpec((step, blocks, ROWS, 2 * (DK + DV)), lambda h: (h, 0, 0, 0)),
            pl.BlockSpec((step, blocks - 1, DK, 2 * (DK + DV)), lambda h: (h, 0, 0, 0)),
            pl.BlockSpec((step, 8 * blocks, ROWS), lambda h: (h, 0, 0)),
        ],
        out_specs=[
            pl.BlockSpec((tok, step * DV), lambda h: (0, h)),
            pl.BlockSpec((tok, step * DK), lambda h: (0, h)),
        ],
        out_shape=[
            jax.ShapeDtypeStruct((tok, heads * DV), F32),
            pltpu.VMEM((tok, heads * DK), F32),
        ],
        compiler_params=pltpu.CompilerParams(dimension_semantics=("arbitrary",)),
        name="query_stage",
    )(queries, keys, solved, prefix, table)


def prefix_kernel(in_ref, ex_ref, end_ref, ends_ref):
    count = in_ref.shape[0]
    flags = [jnp.where(in_ref[i, DK : DK + 1, :] == in_ref[i - 1, DK + 1 : DK + 2, :], 1.0, 0.0)
             for i in range(1, count)]
    maps = [in_ref[i, :DK, :DK] * (1.0 if i == 0 else flags[i - 1][:, :DK]) for i in range(count)]
    adds = [in_ref[i, :DK, DK:] for i in range(count)]
    width = 1
    while width < count:
        new_maps, new_adds = list(maps), list(adds)
        for i in range(count):
            if i & width:
                j = (i // width) * width - 1
                joined = mm(maps[i], jnp.concatenate([maps[j], adds[j]], axis=1))
                new_maps[i] = joined[:, :DK]
                new_adds[i] = joined[:, DK:] + adds[i]
        maps, adds = new_maps, new_adds
        width *= 2
    r, c = iota((DK, DK), 0), iota((DK, DK), 1)
    ex_ref[0, :, :DK] = (r == c).astype(F32)
    ex_ref[0, :, DK:] = jnp.zeros((DK, DV), F32)
    for i in range(1, count):
        ex_ref[i, :, :DK] = maps[i - 1] * flags[i - 1][:, :DK]
        ex_ref[i, :, DK:] = adds[i - 1] * flags[i - 1][:, DK:]
    end_ref[:DK, :] = adds[count - 1]
    end_ref[DK:, :] = in_ref[count - 1, DK:, :DV]
    ends_ref[...] = in_ref[0, DK:, :DV]


def incoming_kernel(ends_ref, ex_ref, end_ref, out_ref):
    flag = jnp.where(ends_ref[0:1, :] == end_ref[DK + 1 : DK + 2, :], 1.0, 0.0)
    state = end_ref[:DK, :] * flag
    for i in range(ex_ref.shape[0]):
        out_ref[i] = mm(ex_ref[i, :, :DK], state) + ex_ref[i, :, DK:]


def far_kernel(place_ref, local_ref, map_ref, state_ref, gain_ref, weight_ref, normed_ref, up_ref, down_ref,
               columns_ref, own_ref, copied, read):
    heads, width = state_ref.shape[0], up_ref.shape[1]
    start = pl.multiple_of(((place_ref[0] + 2) & 3) * width, width)
    bring = pltpu.make_async_copy(local_ref, own_ref, read)
    bring.start()
    load = pltpu.make_async_copy(weight_ref.at[:, pl.ds(start, width)], columns_ref, copied)
    load.start()
    read_out = [mm(map_ref[:, h * DV : (h + 1) * DV], state_ref[h]) for h in range(heads)]
    bring.wait()
    for h in range(heads):
        lanes = slice(h * DV, (h + 1) * DV)
        attended = own_ref[:, lanes] + read_out[h]
        mean = jnp.mean(attended * attended, axis=1, keepdims=True)
        normed_ref[:, lanes] = (attended * lax.rsqrt(mean + EPS) * gain_ref[:, lanes]).astype(BF16)
    load.wait()
    half = up_ref.shape[0]
    terms = dotf(normed_ref[...], columns_ref[...])
    up_ref[...] = terms[:half]
    down_ref[...] = terms[half:]


def tile_kernel(pick_ref, normed_ref, weight_ref, top_ref, bottom_ref):
    half = top_ref.shape[0]
    terms = dotf(normed_ref[...], weight_ref[...])
    top_ref[...] = terms[:half]
    bottom_ref[...] = terms[half:]


def whole(*shape):
    return pl.BlockSpec(shape, lambda i, *_: (0,) * len(shape))


def far_tile(place, local, mapped, state, gain, weight, width):
    tok, feats = local.shape
    part = pltpu.VMEM((tok // 2, width), F32)
    anywhere = pl.BlockSpec(memory_space=pl.ANY)
    return pl.pallas_call(
        far_kernel,
        in_specs=[pl.BlockSpec(memory_space=pltpu.SMEM), anywhere, resident(), resident(), resident(), anywhere],
        out_specs=[resident()] * 3,
        out_shape=[jax.ShapeDtypeStruct((tok, feats), BF16), part, part],
        scratch_shapes=[pltpu.VMEM((feats, width), BF16), pltpu.VMEM((tok, feats), F32),
                        pltpu.SemaphoreType.DMA(()), pltpu.SemaphoreType.DMA(())],
        compiler_params=pltpu.CompilerParams(vmem_limit_bytes=57 << 20),
        name="far_tile",
    )(place, local, held(mapped), held(state), gain.reshape(1, feats), weight)


def join_kernel(nt_ref, gt_ref, lb_ref, gb_ref, top_ref, bottom_ref):
    top_ref[...] = nt_ref[...] + gt_ref[...]
    bottom_ref[...] = lb_ref[...] + gb_ref[...]


def joined(next_top, got_top, last_bottom, got_bottom):
    return pl.pallas_call(
        join_kernel,
        in_specs=[resident()] * 4,
        out_specs=[resident()] * 2,
        out_shape=[pltpu.VMEM(next_top.shape, F32)] * 2,
        compiler_params=pltpu.CompilerParams(vmem_limit_bytes=57 << 20),
        name="join_tiles",
    )(held(next_top), held(got_top), held(last_bottom), held(got_bottom))


def join_kernel(nt_ref, gt_ref, lb_ref, gb_ref, top_ref, bottom_ref):
    top_ref[...] = nt_ref[...] + gt_ref[...]
    bottom_ref[...] = lb_ref[...] + gb_ref[...]


def joined(next_top, got_top, last_bottom, got_bottom):
    return pl.pallas_call(
        join_kernel,
        in_specs=[resident()] * 4,
        out_specs=[resident()] * 2,
        out_shape=[pltpu.VMEM(next_top.shape, F32)] * 2,
        compiler_params=pltpu.CompilerParams(vmem_limit_bytes=57 << 20),
        name="join_tiles",
    )(held(next_top), held(got_top), held(last_bottom), held(got_bottom))


def one_tile(place, normed, weight, width):
    tok, feats = normed.shape
    part = pltpu.VMEM((tok // 2, width), F32)
    cols = width // 2
    out = pl.BlockSpec((tok // 2, cols), lambda i, at: (0, i))
    return pl.pallas_call(
        tile_kernel,
        grid_spec=pltpu.PrefetchScalarGridSpec(
            num_scalar_prefetch=1, grid=(2,),
            in_specs=[whole(tok, feats), pl.BlockSpec((feats, cols), lambda i, at: (0, 2 * at[0] + i))],
            out_specs=[out, out]),
        out_shape=[part, part],
        compiler_params=pltpu.CompilerParams(vmem_limit_bytes=57 << 20),
    )(place, normed, weight)


def sides_kernel(pick_ref, normed_ref, next_w_ref, last_w_ref, nb_ref, lt_ref, nt_ref, lb_ref):
    half = nb_ref.shape[0]
    terms = dotf(normed_ref[...], next_w_ref[...])
    nt_ref[...] = terms[:half]
    nb_ref[...] = terms[half:]
    terms = dotf(normed_ref[...], last_w_ref[...])
    lt_ref[...] = terms[:half]
    lb_ref[...] = terms[half:]


def side_tiles(places, normed, weight, width):
    tok, feats = normed.shape
    steps = 4
    cols = width // steps
    part = jax.ShapeDtypeStruct((tok // 2, width), F32)
    out = pl.BlockSpec((tok // 2, cols), lambda i, at: (0, i))
    return pl.pallas_call(
        sides_kernel,
        grid_spec=pltpu.PrefetchScalarGridSpec(
            num_scalar_prefetch=1, grid=(steps,),
            in_specs=[whole(tok, feats),
                      pl.BlockSpec((feats, cols), lambda i, at: (0, steps * ((at[0] + 1) & 3) + i)),
                      pl.BlockSpec((feats, cols), lambda i, at: (0, steps * ((at[0] + 3) & 3) + i))],
            out_specs=[out] * 4),
        out_shape=[part] * 2 + [pltpu.VMEM((tok // 2, width), F32)] * 2,
        compiler_params=pltpu.CompilerParams(vmem_limit_bytes=57 << 20),
        name="side_tiles",
    )(places, normed, weight, weight)


def finish_kernel(ot_ref, st_ref, gt_ref, ob_ref, sb_ref, gb_ref, out_ref):
    half = ot_ref.shape[0]
    out_ref[:half, :] = (ot_ref[...] + st_ref[...] + gt_ref[...]).astype(BF16)
    out_ref[half:, :] = (ob_ref[...] + sb_ref[...] + gb_ref[...]).astype(BF16)


def summed_output(local, mapped, states, gain, out_weight):
    count = lax.axis_size("head")
    assert count == 4
    mine = lax.axis_index("head")
    width = out_weight.shape[1] // count
    rise = [(i, (i + 1) % count) for i in range(count)]
    fall = [(i, (i - 1) % count) for i in range(count)]
    at = lambda step: ((mine + step) & (count - 1)).astype(jnp.int32).reshape(1)
    up = lambda x: lax.ppermute(x, "head", rise)
    down = lambda x: lax.ppermute(x, "head", fall)
    normed, far_top, far_bottom = far_tile(at(0), local, mapped, states, gain, out_weight, width)
    got_top, got_bottom = up(far_top), down(far_bottom)
    next_bottom, last_top, next_top, last_bottom = side_tiles(
        at(0), normed, out_weight, width)
    side_bottom = up(next_bottom)
    side_top = down(last_top)
    next_top, last_bottom = joined(next_top, got_top, last_bottom, got_bottom)
    got_top, got_bottom = up(next_top), down(last_bottom)
    own_top, own_bottom = one_tile(at(0), normed, out_weight, width)
    return pl.pallas_call(
        finish_kernel,
        in_specs=[resident()] * 6,
        out_shape=jax.ShapeDtypeStruct((2 * own_top.shape[0], width), BF16),
        compiler_params=pltpu.CompilerParams(vmem_limit_bytes=57 << 20),
        name="finish",
    )(*map(held, (own_top, side_top, got_top, own_bottom, side_bottom, got_bottom)))


def shards(queries, keys, values, betas, log_decay, segment, gain, out_weight):
    tok, heads = queries.shape[0], betas.shape[1]
    devices = lax.axis_size("ctx")
    span = DOCUMENT_LIMIT // tok
    assert span == heads and devices % span == 0
    groups = [list(range(i, i + span)) for i in range(0, devices, span)]
    pair, solved, prefix, table = key_stage(keys, values, betas, log_decay, segment)
    local, mapped = query_stage(queries, keys, solved, prefix, table)
    mine = lax.all_to_all(pair, "ctx", 0, 0, axis_index_groups=groups)
    mine, local, mapped = lax.optimization_barrier((mine, local, mapped))
    exclusive, end, ends = pl.pallas_call(
        prefix_kernel,
        in_specs=[resident()],
        out_specs=[resident(), resident(), resident()],
        out_shape=[pltpu.VMEM((span, DK, DK + DV), F32), pltpu.VMEM((DK + 8, DV), F32),
                   pltpu.VMEM((8, DV), F32)],
        compiler_params=pltpu.CompilerParams(vmem_limit_bytes=57 << 20),
        name="prefix_stage",
    )(held(mine))
    end = lax.ppermute(end, "ctx", [(i, i + span) for i in range(devices - span)])
    states = pl.pallas_call(
        incoming_kernel,
        in_specs=[resident(), resident(), resident()],
        out_specs=resident(),
        out_shape=pltpu.VMEM((span, DK, DV), F32),
        compiler_params=pltpu.CompilerParams(vmem_limit_bytes=57 << 20),
        name="incoming_stage",
    )(held(ends), held(exclusive), held(end))
    states = lax.all_to_all(states, "ctx", 0, 0, axis_index_groups=groups)
    return summed_output(local, mapped, states, gain, out_weight)


def solution(mesh):
    return jax.shard_map(
        shards,
        mesh=mesh,
        in_specs=(
            P("ctx", "head"),
            P("ctx", None, "head"),
            P("ctx", None, "head"),
            P(None, "head", "ctx"),
            P("head", "ctx"),
            P("ctx"),
            P("head"),
            P("head", None),
        ),
        out_specs=P("ctx", "head"),
        check_vma=False,
    )
```

```python
import jax
import jax.numpy as jnp
from jax import lax
from jax.experimental import pallas as pl
from jax.experimental.pallas import tpu as pltpu
from jax.sharding import PartitionSpec as P


DK = 128
DV = 128
GROUP = 64
ROWS = 2 * GROUP
DOCUMENT_LIMIT = 2048
EPS = 1e-06
F32 = jnp.float32
BF16 = jnp.bfloat16


def dotf(a, b, dims=(((1,), (0,)), ((), ()))):
    return lax.dot_general(a, b, dims, preferred_element_type=F32)


def halves(x):
    hi = x.astype(BF16)
    lo = (x - hi.astype(F32)).astype(BF16)
    return hi, lo


def side(x):
    return jnp.concatenate(halves(x), axis=1)


def mm(a, b):
    left = side(a)
    outs = []
    for c in range(0, b.shape[1], 128):
        right = side(b[:, c : c + 128])
        r = dotf(left, jnp.concatenate([right, right], axis=0))
        outs.append(r[:, :128] + r[:, 128:])
    return outs[0] if len(outs) == 1 else jnp.concatenate(outs, axis=1)


def mm_tall(a, b):
    m = a.shape[0]
    r = dotf(jnp.concatenate(halves(a), axis=0), side(b))
    return r[:m, :128] + (r[:m, 128:] + r[m:, :128])


def mm_exact_right(a, b16):
    return dotf(side(a), jnp.concatenate([b16, b16], axis=0))


def iota(shape, dim):
    return lax.broadcasted_iota(jnp.int32, shape, dim)


def invert(systems):
    r, c = iota((ROWS, ROWS), 0), iota((ROWS, ROWS), 1)
    eye = (r == c).astype(F32)
    pair = (r >> 1) == (c >> 1)
    xs = [eye - jnp.where(pair, s, 0.0) for s in systems]
    shift = 1
    while (1 << shift) < ROWS:
        band = ((r >> (shift + 1)) == (c >> (shift + 1))) & ((r >> shift) != (c >> shift))
        if shift < 3:
            ys = [mm(jnp.where(band, s, 0.0), x) for s, x in zip(systems, xs)]
            xs = [x - mm(x, y) for x, y in zip(xs, ys)]
        else:
            size = 1 << shift
            low = lambda m: jnp.concatenate(
                [m[i : i + size] for i in range(size, ROWS, 2 * size)], axis=0)

            def spread(m, rest):
                parts = []
                for i in range(ROWS // (2 * size)):
                    parts += [rest(i), m[i * size : (i + 1) * size]]
                return jnp.concatenate(parts, axis=0)

            empty = jnp.zeros((size, ROWS), F32)
            low_band = low(band.astype(F32))
            ys = [mm_tall(low(s) * low_band, x) for s, x in zip(systems, xs)]
            ys = [spread(y, lambda i: empty) for y in ys]
            lows = [low(x) for x in xs]
            lows = [x - mm_tall(x, y) for x, y in zip(lows, ys)]
            xs = [spread(y, lambda i: x[2 * i * size : (2 * i + 1) * size])
                  for x, y in zip(xs, lows)]
        shift += 1
    return xs


def key_kernel(heads_step, blocks, k_ref, v_ref, beta_ref, log_ref, seg_ref,
               pair_ref, solved_ref, prefix_ref, tab_ref):
    step = pl.program_id(0)
    heads = log_ref.shape[0]

    @pl.when(step == 0)
    def _():
        t, s = iota((GROUP, ROWS), 0), iota((GROUP, ROWS), 1)
        even = (s == 2 * t).astype(F32)
        odd = (s == 2 * t + 1).astype(F32)
        upto = (t <= (s >> 1)).astype(F32)
        flat = (t <= s).astype(F32)
        same = (s == t).astype(F32)
        both = even + odd

        def pick(x, sel):
            return lax.dot_general(x, sel, (((1,), (0,)), ((), ())),
                                   precision=lax.Precision.HIGHEST, preferred_element_type=F32)

        def stacked(x):
            return jnp.concatenate([x[:, n * GROUP : (n + 1) * GROUP] for n in range(blocks)], axis=0)

        seg = stacked(jnp.broadcast_to(seg_ref[...].astype(F32), (heads, blocks * GROUP)))
        lg = stacked(log_ref[...])
        kinds = (pick(lg, upto),
                 pick(stacked(beta_ref[0]), even) + pick(stacked(beta_ref[1]), odd),
                 pick(seg, both), pick(lg, flat), pick(seg, same))
        for n in range(blocks):
            for i, kind in enumerate(kinds):
                tab_ref[:, 8 * n + i, :] = kind[n * heads : (n + 1) * heads]
            for z in range(len(kinds), 8):
                tab_ref[:, 8 * n + z, :] = jnp.zeros((heads, ROWS), F32)

    r, c = iota((ROWS, ROWS), 0), iota((ROWS, ROWS), 1)
    diag = r == c
    eye = diag.astype(F32)
    strictly = r > c

    items = []
    for g in range(heads_step):
        lanes = slice(g * DK, (g + 1) * DK)
        table = tab_ref[step * heads_step + g]
        columns = columns_of(table, blocks)
        prior = table[2:3, 0:1]
        for n in range(blocks):
            key = k_ref[n * GROUP : (n + 1) * GROUP, :, lanes].reshape(ROWS, DK)
            value = v_ref[n * GROUP : (n + 1) * GROUP, :, lanes].reshape(ROWS, DV)
            cum_row, beta_row, seg_row = (table[8 * n + i : 8 * n + i + 1] for i in range(3))
            cum_col, beta_col, seg_col = (columns[:, 8 * n + i : 8 * n + i + 1] for i in range(3))
            cum_last, seg_last = cum_row[:, ROWS - 1 :], seg_row[:, ROWS - 1 :]
            raw = dotf(key, key, (((1,), (1,)), ((), ())))
            own = jnp.where(diag, raw, 0.0)
            rk_row = lax.rsqrt(jnp.sum(own, axis=0, keepdims=True) + EPS)
            rk_col = lax.rsqrt(jnp.sum(own, axis=1, keepdims=True) + EPS)
            tab_ref[step * heads_step + g, 8 * n + 5 : 8 * n + 6, :] = rk_row
            system = jnp.where(strictly & (seg_col == seg_row), raw, 0.0) * (
                beta_col * rk_col * jnp.exp(cum_col)) * (rk_row * jnp.exp(-cum_row))
            entry_row = jnp.where(seg_row == prior, jnp.exp(cum_row), 0.0)
            tail_col = jnp.where(seg_col == seg_last, jnp.exp(cum_last - cum_col), 0.0) * rk_col
            tail_entry = jnp.where(seg_last == prior, jnp.exp(cum_last), 0.0)
            items.append(dict(
                g=g, n=n, key=key, value=value, system=system, wv=beta_row,
                wk=beta_row * rk_row * entry_row, tail=tail_col, tail_entry=tail_entry))
            prior = seg_last

    for item, x in zip(items, invert([item["system"] for item in items])):
        item["pseudo"] = mm_exact_right(x * item["wv"], item["value"])
        item["key_mix"] = mm_exact_right(x * item["wk"], item["key"])
    for item in items:
        g, n = item["g"], item["n"]
        both = jnp.concatenate([item["key_mix"], item["pseudo"]], axis=1)
        solved_ref[g, n] = side(both)
        r2 = dotf(item["key"], side(both * item["tail"]), (((0,), (0,)), ((), ())))
        r2 = r2[:, : 2 * DK] + r2[:, 2 * DK :]
        item["pair"] = (item["tail_entry"] * eye - r2[:, :DK], r2[:, DK:])

    def after(later, earlier):
        joined = mm(later[0], jnp.concatenate(earlier, axis=1))
        return joined[:, :DK], joined[:, DK:] + later[1]

    totals = [[items[g * blocks + n]["pair"] for n in range(blocks)] for g in range(heads_step)]
    first, halfway, third = [t[0] for t in totals], [], []
    halfway = [after(t[1], t[0]) for t in totals]
    upper = [after(t[3], t[2]) for t in totals]
    third = [after(t[2], h) for t, h in zip(totals, halfway)]
    final = [after(u, h) for u, h in zip(upper, halfway)]
    begin = seg_ref[:, 0:1].astype(F32)
    last = seg_ref[:, blocks * GROUP - 1 :].astype(F32)
    ends = jnp.where(iota((8, 2 * DK), 0) == 0, begin, last)
    for g in range(heads_step):
        for n, pair in enumerate((first[g], halfway[g], third[g])):
            prefix_ref[g, n] = side(jnp.concatenate(pair, axis=1))
        pair_ref[g, :DK, :DK] = final[g][0]
        pair_ref[g, :DK, DK:] = final[g][1]
        pair_ref[g, DK:, :] = ends


def resident():
    return pl.BlockSpec(memory_space=pltpu.VMEM)


def held(x):
    return pltpu.with_memory_space_constraint(x, pltpu.VMEM)


def columns_of(table, blocks):
    return jnp.concatenate([table, jnp.zeros((ROWS - 8 * blocks, ROWS), F32)], axis=0).T


def mm_sided(a, right):
    width = right.shape[1] // 2
    r = dotf(side(a), jnp.concatenate([right, right], axis=0))
    return r[:, :width] + r[:, width:]


def query_kernel(heads_step, blocks, q_ref, k_ref, solved_ref, prefix_ref, tab_ref, out_ref, map_ref):
    qr, qc = iota((GROUP, ROWS), 0), iota((GROUP, ROWS), 1)
    seen = qc <= 2 * qr + 1
    items = []
    for g in range(heads_step):
        lanes = slice(g * DK, (g + 1) * DK)
        table = tab_ref[g]
        columns = columns_of(table, blocks)
        prior = table[2:3, 0:1]
        for n in range(blocks):
            key = k_ref[n * GROUP : (n + 1) * GROUP, :, lanes].reshape(ROWS, DK)
            query = q_ref[n * GROUP : (n + 1) * GROUP, lanes]
            cum_row, seg_row, rk_row = (table[8 * n + i : 8 * n + i + 1] for i in (0, 2, 5))
            cum_q, seg_q = (columns[:GROUP, 8 * n + i : 8 * n + i + 1] for i in (3, 4))
            raw = dotf(query, key, (((1,), (1,)), ((), ())))
            query32 = query.astype(F32)
            rq = lax.rsqrt(jnp.sum(query32 * query32, axis=1, keepdims=True) + EPS)
            scores = jnp.where(seen & (seg_q == seg_row), raw, 0.0) * (rq * jnp.exp(cum_q)) * (
                rk_row * jnp.exp(-cum_row))
            entry_q = jnp.where(seg_q == prior, jnp.exp(cum_q), 0.0)
            items.append((g, n, query32 * (rq * entry_q), mm_sided(scores, solved_ref[g, n])))
            prior = seg_row[:, ROWS - 1 :]
    for g, n, entering, inner in items:
        rows = slice(n * GROUP, (n + 1) * GROUP)
        lanes = slice(g * DV, (g + 1) * DV)
        reach, local = entering - inner[:, :DK], inner[:, DK:]
        if n:
            joined = mm_sided(reach, prefix_ref[g, n - 1])
            reach, local = joined[:, :DK], local + joined[:, DK:]
        map_ref[rows, lanes] = reach
        out_ref[rows, lanes] = local


KEY_STEP = 4
QUERY_STEP = 2


def key_stage(keys, values, betas, log_decay, segment, step=None):
    tok, heads = keys.shape[0], betas.shape[1]
    blocks = tok // GROUP
    assert blocks == 4
    step = step or KEY_STEP
    body = lambda *refs: key_kernel(step, blocks, *refs)
    return pl.pallas_call(
        body,
        grid=(heads // step,),
        in_specs=[
            pl.BlockSpec((tok, 2, step * DK), lambda h: (0, 0, h)),
            pl.BlockSpec((tok, 2, step * DV), lambda h: (0, 0, h)),
            pl.BlockSpec((2, heads, tok), lambda h: (0, 0, 0)),
            pl.BlockSpec((heads, tok), lambda h: (0, 0)),
            pl.BlockSpec((1, tok), lambda h: (0, 0)),
        ],
        out_specs=[
            pl.BlockSpec((step, DK + 8, DK + DV), lambda h: (h, 0, 0)),
            pl.BlockSpec((step, blocks, ROWS, 2 * (DK + DV)), lambda h: (h, 0, 0, 0)),
            pl.BlockSpec((step, blocks - 1, DK, 2 * (DK + DV)), lambda h: (h, 0, 0, 0)),
            pl.BlockSpec((heads, 8 * blocks, ROWS), lambda h: (0, 0, 0)),
        ],
        out_shape=[
            jax.ShapeDtypeStruct((heads, DK + 8, DK + DV), F32),
            jax.ShapeDtypeStruct((heads, blocks, ROWS, 2 * (DK + DV)), BF16),
            jax.ShapeDtypeStruct((heads, blocks - 1, DK, 2 * (DK + DV)), BF16),
            jax.ShapeDtypeStruct((heads, 8 * blocks, ROWS), F32),
        ],
        compiler_params=pltpu.CompilerParams(dimension_semantics=("arbitrary",)),
        name="key_stage",
    )(keys, values, betas, log_decay, segment.reshape(1, tok))


def query_stage(queries, keys, solved, prefix, table, step=None):
    tok = queries.shape[0]
    heads, blocks = solved.shape[:2]
    step = step or QUERY_STEP
    body = lambda *refs: query_kernel(step, blocks, *refs)
    return pl.pallas_call(
        body,
        grid=(heads // step,),
        in_specs=[
            pl.BlockSpec((tok, step * DK), lambda h: (0, h)),
            pl.BlockSpec((tok, 2, step * DK), lambda h: (0, 0, h)),
            pl.BlockSpec((step, blocks, ROWS, 2 * (DK + DV)), lambda h: (h, 0, 0, 0)),
            pl.BlockSpec((step, blocks - 1, DK, 2 * (DK + DV)), lambda h: (h, 0, 0, 0)),
            pl.BlockSpec((step, 8 * blocks, ROWS), lambda h: (h, 0, 0)),
        ],
        out_specs=[
            pl.BlockSpec((tok, step * DV), lambda h: (0, h)),
            pl.BlockSpec((tok, step * DK), lambda h: (0, h)),
        ],
        out_shape=[
            jax.ShapeDtypeStruct((tok, heads * DV), F32),
            pltpu.VMEM((tok, heads * DK), F32),
        ],
        compiler_params=pltpu.CompilerParams(dimension_semantics=("arbitrary",)),
        name="query_stage",
    )(queries, keys, solved, prefix, table)


def prefix_kernel(in_ref, ex_ref, end_ref, ends_ref):
    count = in_ref.shape[0]
    flags = [jnp.where(in_ref[i, DK : DK + 1, :] == in_ref[i - 1, DK + 1 : DK + 2, :], 1.0, 0.0)
             for i in range(1, count)]
    maps = [in_ref[i, :DK, :DK] * (1.0 if i == 0 else flags[i - 1][:, :DK]) for i in range(count)]
    adds = [in_ref[i, :DK, DK:] for i in range(count)]
    width = 1
    while width < count:
        new_maps, new_adds = list(maps), list(adds)
        for i in range(count):
            if i & width:
                j = (i // width) * width - 1
                joined = mm(maps[i], jnp.concatenate([maps[j], adds[j]], axis=1))
                new_maps[i] = joined[:, :DK]
                new_adds[i] = joined[:, DK:] + adds[i]
        maps, adds = new_maps, new_adds
        width *= 2
    r, c = iota((DK, DK), 0), iota((DK, DK), 1)
    ex_ref[0, :, :DK] = (r == c).astype(F32)
    ex_ref[0, :, DK:] = jnp.zeros((DK, DV), F32)
    for i in range(1, count):
        ex_ref[i, :, :DK] = maps[i - 1] * flags[i - 1][:, :DK]
        ex_ref[i, :, DK:] = adds[i - 1] * flags[i - 1][:, DK:]
    end_ref[:DK, :] = adds[count - 1]
    end_ref[DK:, :] = in_ref[count - 1, DK:, :DV]
    ends_ref[...] = in_ref[0, DK:, :DV]


def incoming_kernel(ends_ref, ex_ref, end_ref, out_ref):
    flag = jnp.where(ends_ref[0:1, :] == end_ref[DK + 1 : DK + 2, :], 1.0, 0.0)
    state = end_ref[:DK, :] * flag
    for i in range(ex_ref.shape[0]):
        out_ref[i] = mm(ex_ref[i, :, :DK], state) + ex_ref[i, :, DK:]


def far_kernel(place_ref, local_ref, map_ref, state_ref, gain_ref, weight_ref, normed_ref, up_ref, down_ref,
               columns_ref, own_ref, copied, read):
    heads, width = state_ref.shape[0], up_ref.shape[1]
    start = pl.multiple_of(((place_ref[0] + 2) & 3) * width, width)
    bring = pltpu.make_async_copy(local_ref, own_ref, read)
    bring.start()
    load = pltpu.make_async_copy(weight_ref.at[:, pl.ds(start, width)], columns_ref, copied)
    load.start()
    read_out = [mm(map_ref[:, h * DV : (h + 1) * DV], state_ref[h]) for h in range(heads)]
    bring.wait()
    for h in range(heads):
        lanes = slice(h * DV, (h + 1) * DV)
        attended = own_ref[:, lanes] + read_out[h]
        mean = jnp.mean(attended * attended, axis=1, keepdims=True)
        normed_ref[:, lanes] = (attended * lax.rsqrt(mean + EPS) * gain_ref[:, lanes]).astype(BF16)
    load.wait()
    half = up_ref.shape[0]
    terms = dotf(normed_ref[...], columns_ref[...])
    up_ref[...] = terms[:half]
    down_ref[...] = terms[half:]


def tile_kernel(pick_ref, normed_ref, weight_ref, top_ref, bottom_ref):
    half = top_ref.shape[0]
    terms = dotf(normed_ref[...], weight_ref[...])
    top_ref[...] = terms[:half]
    bottom_ref[...] = terms[half:]


def whole(*shape):
    return pl.BlockSpec(shape, lambda i, *_: (0,) * len(shape))


def far_tile(place, local, mapped, state, gain, weight, width):
    tok, feats = local.shape
    part = pltpu.VMEM((tok // 2, width), F32)
    anywhere = pl.BlockSpec(memory_space=pl.ANY)
    return pl.pallas_call(
        far_kernel,
        in_specs=[pl.BlockSpec(memory_space=pltpu.SMEM), anywhere, resident(), resident(), resident(), anywhere],
        out_specs=[resident()] * 3,
        out_shape=[jax.ShapeDtypeStruct((tok, feats), BF16), part, part],
        scratch_shapes=[pltpu.VMEM((feats, width), BF16), pltpu.VMEM((tok, feats), F32),
                        pltpu.SemaphoreType.DMA(()), pltpu.SemaphoreType.DMA(())],
        compiler_params=pltpu.CompilerParams(vmem_limit_bytes=57 << 20),
        name="far_tile",
    )(place, local, held(mapped), held(state), gain.reshape(1, feats), weight)


def join_kernel(nt_ref, gt_ref, lb_ref, gb_ref, top_ref, bottom_ref):
    top_ref[...] = nt_ref[...] + gt_ref[...]
    bottom_ref[...] = lb_ref[...] + gb_ref[...]


def joined(next_top, got_top, last_bottom, got_bottom):
    return pl.pallas_call(
        join_kernel,
        in_specs=[resident()] * 4,
        out_specs=[resident()] * 2,
        out_shape=[pltpu.VMEM(next_top.shape, F32)] * 2,
        compiler_params=pltpu.CompilerParams(vmem_limit_bytes=57 << 20),
        name="join_tiles",
    )(held(next_top), held(got_top), held(last_bottom), held(got_bottom))


def join_kernel(nt_ref, gt_ref, lb_ref, gb_ref, top_ref, bottom_ref):
    top_ref[...] = nt_ref[...] + gt_ref[...]
    bottom_ref[...] = lb_ref[...] + gb_ref[...]


def joined(next_top, got_top, last_bottom, got_bottom):
    return pl.pallas_call(
        join_kernel,
        in_specs=[resident()] * 4,
        out_specs=[resident()] * 2,
        out_shape=[pltpu.VMEM(next_top.shape, F32)] * 2,
        compiler_params=pltpu.CompilerParams(vmem_limit_bytes=57 << 20),
        name="join_tiles",
    )(held(next_top), held(got_top), held(last_bottom), held(got_bottom))


def one_tile(place, normed, weight, width):
    tok, feats = normed.shape
    part = pltpu.VMEM((tok // 2, width), F32)
    cols = width // 2
    out = pl.BlockSpec((tok // 2, cols), lambda i, at: (0, i))
    return pl.pallas_call(
        tile_kernel,
        grid_spec=pltpu.PrefetchScalarGridSpec(
            num_scalar_prefetch=1, grid=(2,),
            in_specs=[whole(tok, feats), pl.BlockSpec((feats, cols), lambda i, at: (0, 2 * at[0] + i))],
            out_specs=[out, out]),
        out_shape=[part, part],
        compiler_params=pltpu.CompilerParams(vmem_limit_bytes=57 << 20),
    )(place, normed, weight)


def sides_kernel(pick_ref, normed_ref, next_w_ref, last_w_ref, nb_ref, lt_ref, nt_ref, lb_ref):
    half = nb_ref.shape[0]
    terms = dotf(normed_ref[...], next_w_ref[...])
    nt_ref[...] = terms[:half]
    nb_ref[...] = terms[half:]
    terms = dotf(normed_ref[...], last_w_ref[...])
    lt_ref[...] = terms[:half]
    lb_ref[...] = terms[half:]


def side_tiles(places, normed, weight, width):
    tok, feats = normed.shape
    steps = 4
    cols = width // steps
    part = jax.ShapeDtypeStruct((tok // 2, width), F32)
    out = pl.BlockSpec((tok // 2, cols), lambda i, at: (0, i))
    return pl.pallas_call(
        sides_kernel,
        grid_spec=pltpu.PrefetchScalarGridSpec(
            num_scalar_prefetch=1, grid=(steps,),
            in_specs=[whole(tok, feats),
                      pl.BlockSpec((feats, cols), lambda i, at: (0, steps * ((at[0] + 1) & 3) + i)),
                      pl.BlockSpec((feats, cols), lambda i, at: (0, steps * ((at[0] + 3) & 3) + i))],
            out_specs=[out] * 4),
        out_shape=[part] * 2 + [pltpu.VMEM((tok // 2, width), F32)] * 2,
        compiler_params=pltpu.CompilerParams(vmem_limit_bytes=57 << 20),
        name="side_tiles",
    )(places, normed, weight, weight)


def finish_kernel(ot_ref, st_ref, gt_ref, ob_ref, sb_ref, gb_ref, out_ref):
    @pl.when(pl.program_id(0) == 0)
    def _():
        out_ref[...] = (ot_ref[...] + st_ref[...] + gt_ref[...]).astype(BF16)

    @pl.when(pl.program_id(0) == 1)
    def _():
        out_ref[...] = (ob_ref[...] + sb_ref[...] + gb_ref[...]).astype(BF16)


def summed_output(local, mapped, states, gain, out_weight):
    count = lax.axis_size("head")
    assert count == 4
    mine = lax.axis_index("head")
    width = out_weight.shape[1] // count
    rise = [(i, (i + 1) % count) for i in range(count)]
    fall = [(i, (i - 1) % count) for i in range(count)]
    at = lambda step: ((mine + step) & (count - 1)).astype(jnp.int32).reshape(1)
    up = lambda x: lax.ppermute(x, "head", rise)
    down = lambda x: lax.ppermute(x, "head", fall)
    normed, far_top, far_bottom = far_tile(at(0), local, mapped, states, gain, out_weight, width)
    got_top, got_bottom = up(far_top), down(far_bottom)
    next_bottom, last_top, next_top, last_bottom = side_tiles(
        at(0), normed, out_weight, width)
    side_bottom = up(next_bottom)
    side_top = down(last_top)
    next_top, last_bottom = joined(next_top, got_top, last_bottom, got_bottom)
    got_top, got_bottom = up(next_top), down(last_bottom)
    own_top, own_bottom = one_tile(at(0), normed, out_weight, width)
    return pl.pallas_call(
        finish_kernel,
        grid=(2,),
        in_specs=[resident()] * 6,
        out_specs=pl.BlockSpec(own_top.shape, lambda i: (i, 0)),
        out_shape=jax.ShapeDtypeStruct((2 * own_top.shape[0], width), BF16),
        compiler_params=pltpu.CompilerParams(vmem_limit_bytes=57 << 20),
        name="finish",
    )(*map(held, (own_top, side_top, got_top, own_bottom, side_bottom, got_bottom)))


def shards(queries, keys, values, betas, log_decay, segment, gain, out_weight):
    tok, heads = queries.shape[0], betas.shape[1]
    devices = lax.axis_size("ctx")
    span = DOCUMENT_LIMIT // tok
    assert span == heads and devices % span == 0
    groups = [list(range(i, i + span)) for i in range(0, devices, span)]
    pair, solved, prefix, table = key_stage(keys, values, betas, log_decay, segment)
    local, mapped = query_stage(queries, keys, solved, prefix, table)
    mine = lax.all_to_all(pair, "ctx", 0, 0, axis_index_groups=groups)
    mine, local, mapped = lax.optimization_barrier((mine, local, mapped))
    exclusive, end, ends = pl.pallas_call(
        prefix_kernel,
        in_specs=[resident()],
        out_specs=[resident(), resident(), resident()],
        out_shape=[pltpu.VMEM((span, DK, DK + DV), F32), pltpu.VMEM((DK + 8, DV), F32),
                   pltpu.VMEM((8, DV), F32)],
        compiler_params=pltpu.CompilerParams(vmem_limit_bytes=57 << 20),
        name="prefix_stage",
    )(held(mine))
    end = lax.ppermute(end, "ctx", [(i, i + span) for i in range(devices - span)])
    states = pl.pallas_call(
        incoming_kernel,
        in_specs=[resident(), resident(), resident()],
        out_specs=resident(),
        out_shape=pltpu.VMEM((span, DK, DV), F32),
        compiler_params=pltpu.CompilerParams(vmem_limit_bytes=57 << 20),
        name="incoming_stage",
    )(held(ends), held(exclusive), held(end))
    states = lax.all_to_all(states, "ctx", 0, 0, axis_index_groups=groups)
    return summed_output(local, mapped, states, gain, out_weight)


def solution(mesh):
    return jax.shard_map(
        shards,
        mesh=mesh,
        in_specs=(
            P("ctx", "head"),
            P("ctx", None, "head"),
            P("ctx", None, "head"),
            P(None, "head", "ctx"),
            P("head", "ctx"),
            P("ctx"),
            P("head"),
            P("head", None),
        ),
        out_specs=P("ctx", "head"),
        check_vma=False,
    )
```
